256 devices in a mesh: row: 128 (over y_hi, x, z, core), col: 2 (over y_lo).
Axes of the slice: x: 4, y: 4 (y_hi: 2, y_lo: 2; y = y_hi * 2 + y_lo), z: 8, core: 2. Of those that a mesh axis runs over, the one named last changes fastest.
Arguments:
- activations: bfloat16 [1024, 2048], P('row', 'col'), may hold values from -6 to 6
- out_grad: bfloat16 [1024, 2048], P('row', 'col'), may hold values from -6 to 6
- gate_blocks: bfloat16 [128, 2, 48, 128, 128], P('row', 'col'), may hold values from -0.09375 to 0.09375
- up_blocks: bfloat16 [128, 2, 48, 128, 128], P('row', 'col'), may hold values from -0.09375 to 0.09375
- down_blocks: bfloat16 [128, 2, 48, 128, 128], P('row', 'col'), may hold values from -0.046875 to 0.046875
- block_index: int32 [3, 128, 2, 48], replicated, may hold values from 0 to 56, as said below
- block_dest: int32 [3, 128, 2, 48], P(None, None, 'col'), may hold values from 0 to 192, as said below
Outputs:
- mixed_rows: bfloat16 [1024, 2048], P('row', 'col')
- input_grad: bfloat16 [1024, 2048], P('row', 'col')
- weight_grads: bfloat16 [3, 128, 2, 48, 128, 128], P(None, 'row', 'col')
The draws below stay inside these ranges and needn't reach their ends.
Inputs may be any that keep to these rules, and one draw needn't show every extreme that they name: `block_index`: entries below 56 are live slots; within one list (m, r, c) they are distinct. The value 56 marks an unused slot, placed anywhere in the list. Each list has 8 to 48 live slots; for each matrix some list has exactly 8, and all four lists of some group g and column c have 48. `block_dest`: for a live slot the value is o * 48 + s: its gradient goes to row g * 4 + o of the same group and column, at place s; no two live slots of a group and column share a value; unused slots hold 192. For each matrix some owner's places 0 to 47 are all taken.
All inputs are finite; a program needn't handle non-finite values.
Results may differ from the reference program's by a relative error of at most 0.0049.
Values may be sent and summed in bfloat16 or wider, within the bound.
No kernel may reach another device: no remote copies, remote signals or barrier semaphores. Data moves between devices by JAX's collectives and lax.ppermute only.
A program may use at most 192 MiB of HBM per device.

```python
import jax
import jax.numpy as jnp
from jax import lax

D = 8192
FF = 28672
BLK = 128
QUARTERS = 4
TOKENS = 256
GROUPS = 32
TG = 8
DQ = 1024
FB = 7
DB = 8
SLOTS = 56
CAP = 48
MINB = 8
N_ROW = 128
N_COL = 2


def block_layout(key):
    base_key = jax.random.fold_in(key, 11)
    keys = jax.random.split(base_key, 6)
    group_total = N_ROW // QUARTERS
    counts = jax.random.randint(keys[0], (3, group_total, N_COL, QUARTERS), MINB, CAP + 1)
    full_group = jax.random.randint(keys[1], (3,), 0, group_total)
    full_col = jax.random.randint(keys[2], (3,), 0, N_COL)
    group_ids = jnp.arange(group_total, dtype=jnp.int32)[None, :, None, None]
    col_ids = jnp.arange(N_COL, dtype=jnp.int32)[None, None, :, None]
    quarter_ids = jnp.arange(QUARTERS, dtype=jnp.int32)[None, None, None, :]
    same_col = col_ids == full_col[:, None, None, None]
    is_full = (group_ids == full_group[:, None, None, None]) & same_col
    low_group = (full_group + 1) % group_total
    is_low = (group_ids == low_group[:, None, None, None]) & same_col & (quarter_ids == 0)
    counts = jnp.where(is_full, CAP, jnp.where(is_low, MINB, counts))
    slot_scores = jax.random.randint(keys[3], (3, group_total, N_COL, QUARTERS, SLOTS), 0, 2 ** 20)
    slot_scores = slot_scores * SLOTS + jnp.arange(SLOTS, dtype=jnp.int32)
    candidates = jnp.argsort(slot_scores, axis=-1)[..., :CAP].astype(jnp.int32)
    live_first = jnp.arange(CAP, dtype=jnp.int32) < counts[..., None]
    index_first = jnp.where(live_first, candidates, SLOTS)
    shuffle_scores = jax.random.randint(keys[4], (3, group_total, N_COL, QUARTERS, CAP), 0, 2 ** 20)
    shuffle_scores = shuffle_scores * CAP + jnp.arange(CAP, dtype=jnp.int32)
    shuffle_order = jnp.argsort(shuffle_scores, axis=-1)
    index_list = jnp.take_along_axis(index_first, shuffle_order, axis=-1)
    live_group = (index_list < SLOTS).reshape(3, group_total, N_COL, QUARTERS * CAP)
    owner_scores = jax.random.randint(keys[5], (3, group_total, N_COL, QUARTERS * CAP), 0, 2 ** 20)
    owner_scores = jnp.where(live_group, owner_scores, 2 ** 20)
    owner_scores = owner_scores * (QUARTERS * CAP) + jnp.arange(QUARTERS * CAP, dtype=jnp.int32)
    ranked_order = jnp.argsort(owner_scores, axis=-1)
    rank_slot = jnp.argsort(ranked_order, axis=-1).astype(jnp.int32)
    dest_list = jnp.where(live_group, rank_slot % QUARTERS * CAP + rank_slot // QUARTERS, QUARTERS * CAP)
    dest_list = dest_list.reshape(3, group_total, N_COL, QUARTERS, CAP)
    index_out = index_list.transpose(0, 1, 3, 2, 4).reshape(3, N_ROW, N_COL, CAP)
    dest_out = dest_list.transpose(0, 1, 3, 2, 4).reshape(3, N_ROW, N_COL, CAP)
    return (index_out.astype(jnp.int32), dest_out.astype(jnp.int32))


def draw_block_index(key, part):
    return block_layout(key)[0]


def draw_block_dest(key, part):
    return block_layout(key)[1]


def steps_of(rng, dims, shards, smallest, high):
    level = 1.0
    for dim, blocks in shards:
        steps = jax.random.uniform(jax.random.fold_in(jax.random.fold_in(rng, 6), dim), (blocks,), jnp.float32, smallest / len(shards), high / len(shards))
        level = level * jnp.repeat(jnp.exp(steps), dims[dim] // blocks).reshape((-1,) + (1,) * (len(dims) - 1 - dim))
    return level


def scatter_about(key, extent, deviation, limit, cuts=(), held_as=jnp.bfloat16):
    array = jax.random.normal(key, extent, jnp.float32) * deviation
    if len(cuts) > 0:
        array = steps_of(key, extent, cuts, -0.22, 0.18) * array
    return jnp.clip(array, min=-limit, max=limit).astype(held_as)


def setup_inputs(seed: int = 0) -> dict:
    key_list = jax.random.split(jax.random.key(seed), 8)
    activations = scatter_about(key_list[0], (GROUPS * QUARTERS * TG, N_COL * DQ), 1.0, 6.0, ((0, 128), (1, 2)))
    out_grad = scatter_about(key_list[1], (GROUPS * QUARTERS * TG, N_COL * DQ), 1.0, 6.0, ((0, 128), (1, 2)))
    gate_blocks = scatter_about(key_list[2], (GROUPS * QUARTERS, N_COL, CAP, BLK, BLK), (D // 2) ** -0.5, 0.09375, ((0, 128), (1, 2)))
    up_blocks = scatter_about(key_list[3], (GROUPS * QUARTERS, N_COL, CAP, BLK, BLK), (D // 2) ** -0.5, 0.09375, ((0, 128), (1, 2)))
    down_blocks = scatter_about(key_list[4], (GROUPS * QUARTERS, N_COL, CAP, BLK, BLK), (FF // 2) ** -0.5, 0.046875, ((0, 128), (1, 2)))
    block_index = draw_block_index(jax.random.fold_in(key_list[7], 71), 0)
    block_dest = draw_block_dest(jax.random.fold_in(key_list[7], 71), 0)
    return {"activations": activations, "out_grad": out_grad, "gate_blocks": gate_blocks, "up_blocks": up_blocks, "down_blocks": down_blocks, "block_index": block_index, "block_dest": block_dest}


def unpack_rows(packed):
    shaped = packed.reshape(GROUPS, QUARTERS, TG, N_COL, DQ)
    return shaped.transpose(0, 2, 3, 1, 4).reshape(TOKENS, D)


def pack_rows(full_rows):
    shaped = full_rows.reshape(GROUPS, TG, N_COL, QUARTERS, DQ)
    return shaped.transpose(0, 3, 1, 2, 4).reshape(GROUPS * QUARTERS * TG, N_COL * DQ)


def block_places(index_list):
    row_ids = jnp.arange(N_ROW, dtype=jnp.int32)[:, None, None]
    col_ids = jnp.arange(N_COL, dtype=jnp.int32)[None, :, None]
    live_slots = index_list < SLOTS
    hidden_ids = (row_ids // QUARTERS) * FB + index_list // DB
    feature_ids = (col_ids * QUARTERS + row_ids % QUARTERS) * DB + index_list % DB
    return live_slots, hidden_ids, feature_ids


def features_first(blocks, live_slots, hidden_ids, feature_ids):
    flat_blocks = blocks.reshape(-1, BLK, BLK)
    hidden_flat = jnp.where(live_slots, hidden_ids, FF // BLK).reshape(-1)
    feature_flat = jnp.where(live_slots, feature_ids, D // BLK).reshape(-1)
    block_grid = jnp.zeros((D // BLK, BLK, FF // BLK, BLK), blocks.dtype)
    block_grid = block_grid.at[feature_flat, :, hidden_flat, :].set(flat_blocks, mode="drop")
    return block_grid.reshape(D, FF)


def hidden_first(blocks, live_slots, hidden_ids, feature_ids):
    flat_blocks = blocks.reshape(-1, BLK, BLK)
    hidden_flat = jnp.where(live_slots, hidden_ids, FF // BLK).reshape(-1)
    feature_flat = jnp.where(live_slots, feature_ids, D // BLK).reshape(-1)
    block_grid = jnp.zeros((FF // BLK, BLK, D // BLK, BLK), blocks.dtype)
    block_grid = block_grid.at[hidden_flat, :, feature_flat, :].set(flat_blocks, mode="drop")
    return block_grid.reshape(FF, D)


def block_grads(left_rows, right_rows, left_ids, right_ids):
    left_last = left_rows.shape[1] - 1
    right_last = right_rows.shape[1] - 1

    def one_list(id_pair):
        left_part = jnp.take(left_rows, jnp.minimum(id_pair[0], left_last), axis=1).astype(jnp.float32)
        right_part = jnp.take(right_rows, jnp.minimum(id_pair[1], right_last), axis=1).astype(jnp.float32)
        return jnp.einsum("tkx,tky->kxy", left_part, right_part).astype(jnp.bfloat16)

    listed = (left_ids.reshape(N_ROW * N_COL, CAP), right_ids.reshape(N_ROW * N_COL, CAP))
    return lax.map(one_list, listed).reshape(N_ROW, N_COL, CAP, BLK, BLK)


def reference(activations, out_grad, gate_blocks, up_blocks, down_blocks, block_index, block_dest):
    inputs = unpack_rows(activations)
    upstream = unpack_rows(out_grad)
    gate_live, gate_hidden, gate_feature = block_places(block_index[0])
    up_live, up_hidden, up_feature = block_places(block_index[1])
    down_live, down_hidden, down_feature = block_places(block_index[2])
    w_gate = features_first(gate_blocks, gate_live, gate_hidden, gate_feature)
    w_up = features_first(up_blocks, up_live, up_hidden, up_feature)
    w_down = hidden_first(down_blocks, down_live, down_hidden, down_feature)
    gate_sum = jnp.dot(inputs, w_gate, preferred_element_type=jnp.float32)
    up_sum = jnp.dot(inputs, w_up, preferred_element_type=jnp.float32)
    sigmoid_gate = jax.nn.sigmoid(gate_sum)
    silu_gate = gate_sum * sigmoid_gate
    hidden = (silu_gate * up_sum).astype(jnp.bfloat16)
    mixed_out = jnp.dot(hidden, w_down, preferred_element_type=jnp.float32).astype(jnp.bfloat16)
    contract_last = (((1,), (1,)), ((), ()))
    hidden_grad = lax.dot_general(upstream, w_down, contract_last, preferred_element_type=jnp.float32)
    gate_grad = (hidden_grad * up_sum * sigmoid_gate * (1.0 + gate_sum * (1.0 - sigmoid_gate))).astype(jnp.bfloat16)
    up_grad = (hidden_grad * silu_gate).astype(jnp.bfloat16)
    input_sum = lax.dot_general(gate_grad, w_gate, contract_last, preferred_element_type=jnp.float32)
    input_sum = input_sum + lax.dot_general(up_grad, w_up, contract_last, preferred_element_type=jnp.float32)
    input_grad = input_sum.astype(jnp.bfloat16)
    input_blocks = inputs.reshape(TOKENS, D // BLK, BLK)
    upstream_blocks = upstream.reshape(TOKENS, D // BLK, BLK)
    hidden_blocks = hidden.reshape(TOKENS, FF // BLK, BLK)
    grad_list = (
        block_grads(input_blocks, gate_grad.reshape(TOKENS, FF // BLK, BLK), gate_feature, gate_hidden),
        block_grads(input_blocks, up_grad.reshape(TOKENS, FF // BLK, BLK), up_feature, up_hidden),
        block_grads(hidden_blocks, upstream_blocks, down_hidden, down_feature),
    )
    row_ids = jnp.arange(N_ROW, dtype=jnp.int32)[:, None, None]
    col_ids = jnp.arange(N_COL, dtype=jnp.int32)[None, :, None]
    weight_grads = jnp.zeros((3, N_ROW, N_COL, CAP, BLK, BLK), jnp.bfloat16)
    for matrix in range(3):
        live_slots = block_index[matrix] < SLOTS
        owner_row = (row_ids // QUARTERS) * QUARTERS + block_dest[matrix] // CAP
        owner_row = jnp.where(live_slots, owner_row, N_ROW)
        place_ids = block_dest[matrix] % CAP
        col_full = jnp.broadcast_to(col_ids, owner_row.shape)
        weight_grads = weight_grads.at[matrix, owner_row, col_full, place_ids].set(grad_list[matrix], mode="drop")
    return (pack_rows(mixed_out), pack_rows(input_grad), weight_grads)
```

```python
import functools

import jax
import jax.numpy as jnp
from jax import lax
from jax.experimental import pallas as pl
from jax.experimental.pallas import tpu as pltpu
from jax.sharding import PartitionSpec as P

BLK = 128
QUARTERS = 4
FB = 7
DB = 8
SLOTS = 56
CAP = 48
DQ = 1024
HB = 896
TG = 8
GROUPS = 32
TOKENS = 256
BF = jnp.bfloat16
F32 = jnp.float32
NT = (((1,), (1,)), ((), ()))
VMEM = pl.BlockSpec(memory_space=pltpu.VMEM)
SMEM = pl.BlockSpec(memory_space=pltpu.SMEM)
ANY = pl.BlockSpec(memory_space=pl.ANY)


def row_swap(value, mask):
    return lax.ppermute(value, "row", [(i, i ^ mask) for i in range(128)])


def square_swap(value, step):
    mask = (step >> 1) * 4 | (step & 1)
    return lax.ppermute(value, ("row", "col"), [(i, i ^ mask) for i in range(256)])


def deep_mask(step):
    return (step & 3) << 2 | (step >> 2) << 6


def x_mask(step):
    return step << 4


def sds(shape, dtype):
    return jax.ShapeDtypeStruct(shape, dtype)


def call(kernel, out_shape, in_specs, out_specs=None, scratch=(), limit=40, cost=None):
    many = isinstance(out_shape, (tuple, list))
    if out_specs is None:
        out_specs = [VMEM] * len(out_shape) if many else VMEM
    return pl.pallas_call(
        kernel,
        out_shape=out_shape,
        in_specs=in_specs,
        out_specs=out_specs,
        scratch_shapes=list(scratch),
        compiler_params=pltpu.CompilerParams(vmem_limit_bytes=limit * 2**20),
        cost_estimate=cost,
    )


def dense_kernel(index_ref, gate_ref, up_ref, down_ref, wg_ref, wu_ref, wd_ref, sems):
    wg_ref[...] = jnp.zeros_like(wg_ref)
    wu_ref[...] = jnp.zeros_like(wu_ref)
    wd_ref[...] = jnp.zeros_like(wd_ref)

    def each(act):
        def one(slot, carry):
            for m, (blocks, dense) in enumerate(
                ((gate_ref, wg_ref), (up_ref, wu_ref), (down_ref, wd_ref))
            ):
                place = index_ref[m, slot]

                @pl.when(place < SLOTS)
                def _():
                    hid = pl.multiple_of(place // DB * BLK, BLK)
                    feat = pl.multiple_of(place % DB * BLK, BLK)
                    first, second = (hid, feat) if m == 2 else (feat, hid)
                    act(
                        pltpu.make_async_copy(
                            blocks.at[slot],
                            dense.at[pl.ds(first, BLK), pl.ds(second, BLK)],
                            sems.at[m, slot],
                        )
                    )

            return carry

        lax.fori_loop(0, CAP, one, 0)

    each(lambda copy: copy.start())
    each(lambda copy: copy.wait())


def partial_kernel(place_ref, p0, p1, p2, p3, wg_ref, wu_ref, wd_ref, keep_ref, send_ref, rows):
    core = place_ref[0]
    first = pl.multiple_of(core * 128, 128)
    second = pl.multiple_of((1 - core) * 128, 128)
    rows[pl.ds(first, 64), :] = p0[...]
    rows[pl.ds(first + 64, 64), :] = p1[...]
    rows[pl.ds(second, 64), :] = p2[...]
    rows[pl.ds(second + 64, 64), :] = p3[...]
    x = rows[:, :DQ]
    dy = rows[:, DQ:]
    for at, value in (
        (0, lambda: jnp.dot(x, wg_ref[...], preferred_element_type=F32)),
        (1, lambda: jnp.dot(x, wu_ref[...], preferred_element_type=F32)),
        (2, lambda: lax.dot_general(dy, wd_ref[...], NT, preferred_element_type=F32)),
    ):
        part = value()
        keep_ref[:, at * HB : (at + 1) * HB] = part[:128]
        send_ref[:, at * HB : (at + 1) * HB] = part[128:]


def pair_kernel(place_ref, keep_ref, got_ref, o0, o1, o2, o3):
    me = place_ref[1]
    for step, out in enumerate((o0, o1, o2, o3)):
        at = pl.ds(pl.multiple_of((me ^ step) * 32, 32), 32)
        out[...] = keep_ref[at, :] + got_ref[at, :]


def act_kernel(a0, a1, a2, a3, out_ref):
    def total(at):
        part = slice(at * HB, (at + 1) * HB)
        return (a0[:, part] + a1[:, part]) + (a2[:, part] + a3[:, part])

    gate, up, dh = total(0), total(1), total(2)
    sig = jax.nn.sigmoid(gate)
    silu = gate * sig
    out_ref[:, :HB] = (silu * up).astype(BF)
    out_ref[:, HB : 2 * HB] = (dh * up * sig * (1.0 + gate * (1.0 - sig))).astype(BF)
    out_ref[:, 2 * HB :] = (dh * silu).astype(BF)


def spread(place_ref, mine, theirs, rows):
    core, me = place_ref[0], place_ref[1]
    for step in range(4):
        at = pl.multiple_of(core * 128 + (me ^ step) * 32, 32)
        rows[pl.ds(at, 32), :] = mine[step * 32 : (step + 1) * 32, :]
        at = pl.multiple_of((1 - core) * 128 + (me ^ step) * 32, 32)
        rows[pl.ds(at, 32), :] = theirs[step * 32 : (step + 1) * 32, :]


def out_kernel(place_ref, mine, theirs, wg_ref, wu_ref, wd_ref, t0, t1, t2, t3, full_ref):
    spread(place_ref, mine, theirs, full_ref)
    mixed = jnp.dot(full_ref[:, :HB], wd_ref[...], preferred_element_type=F32)
    for step, out in enumerate((t0, t1, t2, t3)):
        out[:, :DQ] = mixed[step * 64 : (step + 1) * 64].astype(out.dtype)
    grad = lax.dot_general(full_ref[:, HB : 2 * HB], wg_ref[...], NT, preferred_element_type=F32)
    grad += lax.dot_general(full_ref[:, 2 * HB :], wu_ref[...], NT, preferred_element_type=F32)
    for step, out in enumerate((t0, t1, t2, t3)):
        out[:, DQ:] = grad[step * 64 : (step + 1) * 64].astype(out.dtype)


def prep_kernel(p0, p1, p2, p3, xt_ref, dy_ref, rows):
    for step, piece in enumerate((p0, p1, p2, p3)):
        rows[step * 64 : (step + 1) * 64, :] = piece[...]
    for b in range(DB):
        xt_ref[b] = rows[:, b * BLK : (b + 1) * BLK].T
        dy_ref[b] = rows[:, DQ + b * BLK : DQ + (b + 1) * BLK]


def grad_kernel(code_ref, full_ref, x0, x1, x2, x3, y0, y1, y2, y3, out_ref, xt, dy, ht, dg, du):
    for j, (x, y) in enumerate(((x0, y0), (x1, y1), (x2, y2), (x3, y3))):
        xt[j * DB : (j + 1) * DB] = x[...]
        dy[j * DB : (j + 1) * DB] = y[...]
    for a in range(FB):
        ht[a] = full_ref[:, a * BLK : (a + 1) * BLK].T
        dg[a] = full_ref[:, HB + a * BLK : HB + (a + 1) * BLK]
        du[a] = full_ref[:, 2 * HB + a * BLK : 2 * HB + (a + 1) * BLK]

    def one(slot, carry):
        for m in range(3):
            code = code_ref[m, slot]

            @pl.when(code > 0)
            def _():
                where = code - 1
                feat = where // 64 * DB + where % 8
                hid = where % 64 // 8
                left, right = ((xt.at[feat], dg.at[hid]), (xt.at[feat], du.at[hid]), (ht.at[hid], dy.at[feat]))[m]
                out_ref[m, slot] = jnp.dot(left[...], right[...], preferred_element_type=F32).astype(BF)

            @pl.when(code == 0)
            def _():
                out_ref[m, slot] = jnp.zeros((BLK, BLK), BF)

        return carry

    lax.fori_loop(0, CAP, one, 0)


def body(activations, out_grad, gate_blocks, up_blocks, down_blocks, block_index, block_dest):
    row = lax.axis_index("row")
    col = lax.axis_index("col")
    group = row // QUARTERS
    quarter = row % QUARTERS
    place = jnp.stack([row % 2, row // 2 % 2 * 2 + col]).astype(jnp.int32)
    all_index = lax.dynamic_index_in_dim(block_index, col, axis=2, keepdims=False)
    own_index = lax.dynamic_index_in_dim(all_index, row, axis=1, keepdims=False)

    shard = jnp.concatenate([activations, out_grad], axis=1)
    near = jnp.concatenate([shard] + [row_swap(shard, deep_mask(i)) for i in range(1, 8)], axis=0)
    pieces = [near] + [row_swap(near, x_mask(i)) for i in range(1, 4)]
    wide = [sds((DQ, HB), BF), sds((DQ, HB), BF), sds((HB, DQ), BF)]
    wg, wu, wd = call(
        dense_kernel, wide, [SMEM, ANY, ANY, ANY], scratch=[pltpu.SemaphoreType.DMA((3, CAP))], limit=24
    )(
        own_index,
        gate_blocks.reshape(CAP, BLK, BLK),
        up_blocks.reshape(CAP, BLK, BLK),
        down_blocks.reshape(CAP, BLK, BLK),
    )

    half = sds((128, 3 * HB), F32)
    keep, send = call(
        partial_kernel, [half, half], [SMEM] + [VMEM] * 7, scratch=[pltpu.VMEM((TOKENS, 2 * DQ), BF)]
    )(place, *pieces, wg, wu, wd)
    got = row_swap(send, 1)
    fours = call(pair_kernel, [sds((32, 3 * HB), F32)] * 4, [SMEM, VMEM, VMEM])(place, keep, got)
    sums = [fours[0]] + [square_swap(fours[i], i) for i in range(1, 4)]
    share = call(act_kernel, sds((32, 3 * HB), BF), [VMEM] * 4)(*sums)
    mine = jnp.concatenate([share] + [square_swap(share, i) for i in range(1, 4)], axis=0)
    theirs = row_swap(mine, 1)
    outs = call(
        out_kernel,
        [sds((64, 2 * DQ), F32)] + [sds((64, 2 * DQ), BF)] * 3 + [sds((TOKENS, 3 * HB), BF)],
        [SMEM] + [VMEM] * 5,
    )(place, mine, theirs, wg, wu, wd)
    full = outs[4]
    far = outs[0]
    for i in range(1, 4):
        far = far + row_swap(outs[i], x_mask(i)).astype(F32)
    last = far[:TG]
    for i in range(1, 8):
        last = last + row_swap(far[i * TG : (i + 1) * TG].astype(BF), deep_mask(i)).astype(F32)
    last = last.astype(BF)

    mirror = row_swap(near, 2)
    mirrors = [mirror] + [row_swap(mirror, x_mask(i)) for i in range(1, 4)]
    prepped = [sds((DB, BLK, TOKENS), BF), sds((DB, TOKENS, BLK), BF)]
    prep = call(prep_kernel, prepped, [VMEM] * 4, scratch=[pltpu.VMEM((TOKENS, 2 * DQ), BF)])
    x0, y0 = prep(*pieces)
    x2, y2 = prep(*mirrors)
    x1, y1, x3, y3 = [row_swap(v, 1) for v in (x0, y0, x2, y2)]

    dest = lax.dynamic_slice_in_dim(block_dest[:, :, 0, :], group * QUARTERS, QUARTERS, axis=1)
    index = lax.dynamic_slice_in_dim(all_index, group * QUARTERS, QUARTERS, axis=1)
    swap = (jnp.arange(QUARTERS, dtype=jnp.int32) ^ quarter)[None, :, None]
    value = (swap * 64 + index + 1).reshape(3, 1, QUARTERS * CAP)
    targets = quarter * CAP + jnp.arange(CAP, dtype=jnp.int32)
    hits = dest.reshape(3, 1, QUARTERS * CAP) == targets[None, :, None]
    code = jnp.sum(jnp.where(hits, value, 0), axis=2, dtype=jnp.int32)

    grads = call(
        grad_kernel,
        sds((3, CAP, BLK, BLK), BF),
        [SMEM] + [VMEM] * 9,
        scratch=[
            pltpu.VMEM((QUARTERS * DB, BLK, TOKENS), BF),
            pltpu.VMEM((QUARTERS * DB, TOKENS, BLK), BF),
            pltpu.VMEM((FB, BLK, TOKENS), BF),
            pltpu.VMEM((FB, TOKENS, BLK), BF),
            pltpu.VMEM((FB, TOKENS, BLK), BF),
        ],
    )(code, full, x0, x1, x2, x3, y0, y1, y2, y3)
    return last[:, :DQ], last[:, DQ:], grads.reshape(3, 1, 1, CAP, BLK, BLK)


def solution(mesh):
    return jax.shard_map(
        body,
        mesh=mesh,
        in_specs=(
            P("row", "col"),
            P("row", "col"),
            P("row", "col", None, None, None),
            P("row", "col", None, None, None),
            P("row", "col", None, None, None),
            P(),
            P(None, None, "col", None),
        ),
        out_specs=(P("row", "col"), P("row", "col"), P(None, "row", "col", None, None, None)),
        check_vma=False,
    )
```

```python
import functools

import jax
import jax.numpy as jnp
from jax import lax
from jax.experimental import pallas as pl
from jax.experimental.pallas import tpu as pltpu
from jax.sharding import PartitionSpec as P

BLK = 128
QUARTERS = 4
FB = 7
DB = 8
SLOTS = 56
CAP = 48
DQ = 1024
HB = 896
TG = 8
STEP = 8
TOKENS = 256
BF = jnp.bfloat16
F32 = jnp.float32
NT = (((1,), (1,)), ((), ()))
VMEM = pl.BlockSpec(memory_space=pltpu.VMEM)
SMEM = pl.BlockSpec(memory_space=pltpu.SMEM)


def row_swap(value, mask):
    return lax.ppermute(value, "row", [(i, i ^ mask) for i in range(128)])


def square_swap(value, step):
    mask = (step >> 1) * 4 | (step & 1)
    return lax.ppermute(value, ("row", "col"), [(i, i ^ mask) for i in range(256)])


def z_mask(step):
    return step << 2


Y_MASK = 64


def x_mask(step):
    return step << 4


def sds(shape, dtype):
    return jax.ShapeDtypeStruct(shape, dtype)


def call(kernel, out_shape, in_specs, out_specs=None, scratch=(), limit=16, grid=()):
    many = isinstance(out_shape, (tuple, list))
    if out_specs is None:
        out_specs = [VMEM] * len(out_shape) if many else VMEM
    return pl.pallas_call(
        kernel,
        out_shape=out_shape,
        in_specs=in_specs,
        out_specs=out_specs,
        grid=grid,
        scratch_shapes=list(scratch),
        compiler_params=pltpu.CompilerParams(vmem_limit_bytes=limit * 2**20),
    )


def dense_kernel(index_ref, gate_ref, up_ref, down_ref, wg_ref, wu_ref, wd_ref):
    wg_ref[...] = jnp.zeros_like(wg_ref)
    wu_ref[...] = jnp.zeros_like(wu_ref)
    wd_ref[...] = jnp.zeros_like(wd_ref)

    def one(slot, carry):
        for m, (blocks, dense) in enumerate(((gate_ref, wg_ref), (up_ref, wu_ref), (down_ref, wd_ref))):
            place = index_ref[m, slot]

            @pl.when(place < SLOTS)
            def _():
                hid = pl.multiple_of(place // DB * BLK, BLK)
                feat = pl.multiple_of(place % DB * BLK, BLK)
                first, second = (hid, feat) if m == 2 else (feat, hid)
                dense[pl.ds(first, BLK), pl.ds(second, BLK)] = blocks[slot]

        return carry

    lax.fori_loop(0, CAP, one, 0)


def partial_kernel(place_ref, p0, p1, p2, p3, wg_ref, wu_ref, wd_ref, keep_ref, send_ref, rows):
    core = place_ref[0]
    first = pl.multiple_of(core * 128, 128)
    second = pl.multiple_of((1 - core) * 128, 128)
    rows[pl.ds(first, 64), :] = p0[...]
    rows[pl.ds(first + 64, 64), :] = p1[...]
    rows[pl.ds(second, 64), :] = p2[...]
    rows[pl.ds(second + 64, 64), :] = p3[...]
    x = rows[:, :DQ]
    dy = rows[:, DQ:]
    for at, value in (
        (0, lambda: jnp.dot(x, wg_ref[...], preferred_element_type=F32)),
        (1, lambda: jnp.dot(x, wu_ref[...], preferred_element_type=F32)),
        (2, lambda: lax.dot_general(dy, wd_ref[...], NT, preferred_element_type=F32)),
    ):
        part = value()
        keep_ref[:, at * HB : (at + 1) * HB] = part[:128]
        send_ref[:, at * HB : (at + 1) * HB] = part[128:]


def pair_kernel(place_ref, keep_ref, got_ref, o0, o1, o2, o3):
    me = place_ref[1]
    for step, out in enumerate((o0, o1, o2, o3)):
        at = pl.ds(pl.multiple_of((me ^ step) * 32, 32), 32)
        out[...] = keep_ref[at, :] + got_ref[at, :]


def act_kernel(a0, a1, a2, a3, out_ref):
    def total(at):
        part = slice(at * HB, (at + 1) * HB)
        return (a0[:, part] + a1[:, part]) + (a2[:, part] + a3[:, part])

    gate, up, dh = total(0), total(1), total(2)
    sig = jax.nn.sigmoid(gate)
    silu = gate * sig
    out_ref[:, :HB] = (silu * up).astype(BF)
    out_ref[:, HB : 2 * HB] = (dh * up * sig * (1.0 + gate * (1.0 - sig))).astype(BF)
    out_ref[:, 2 * HB :] = (dh * silu).astype(BF)


def spread(place_ref, mine, theirs, rows):
    core, me = place_ref[0], place_ref[1]
    for step in range(4):
        at = pl.multiple_of(core * 128 + (me ^ step) * 32, 32)
        rows[pl.ds(at, 32), :] = mine[step * 32 : (step + 1) * 32, :]
        at = pl.multiple_of((1 - core) * 128 + (me ^ step) * 32, 32)
        rows[pl.ds(at, 32), :] = theirs[step * 32 : (step + 1) * 32, :]


def out_kernel(place_ref, mine, theirs, wg_ref, wu_ref, wd_ref, t0, t1, t2, t3, full_ref):
    spread(place_ref, mine, theirs, full_ref)
    mixed = jnp.dot(full_ref[:, :HB], wd_ref[...], preferred_element_type=F32)
    for step, out in enumerate((t0, t1, t2, t3)):
        out[:, :DQ] = mixed[step * 64 : (step + 1) * 64].astype(out.dtype)
    grad = lax.dot_general(full_ref[:, HB : 2 * HB], wg_ref[...], NT, preferred_element_type=F32)
    grad += lax.dot_general(full_ref[:, 2 * HB :], wu_ref[...], NT, preferred_element_type=F32)
    for step, out in enumerate((t0, t1, t2, t3)):
        out[:, DQ:] = grad[step * 64 : (step + 1) * 64].astype(out.dtype)


def prep_kernel(p0, p1, p2, p3, xt_ref, dy_ref, rows):
    for step, piece in enumerate((p0, p1, p2, p3)):
        rows[step * 64 : (step + 1) * 64, :] = piece[...]
    for b in range(DB):
        xt_ref[b] = rows[:, b * BLK : (b + 1) * BLK].T
        dy_ref[b] = rows[:, DQ + b * BLK : DQ + (b + 1) * BLK]


def grad_kernel(code_ref, full_ref, x0, x1, x2, x3, y0, y1, y2, y3, out_ref, xt, dy, ht, dg, du):
    turn = pl.program_id(0)

    @pl.when(turn == 0)
    def _():
        for j, (x, y) in enumerate(((x0, y0), (x1, y1), (x2, y2), (x3, y3))):
            xt[j * DB : (j + 1) * DB] = x[...]
            dy[j * DB : (j + 1) * DB] = y[...]
        for a in range(FB):
            ht[a] = full_ref[:, a * BLK : (a + 1) * BLK].T
            dg[a] = full_ref[:, HB + a * BLK : HB + (a + 1) * BLK]
            du[a] = full_ref[:, 2 * HB + a * BLK : 2 * HB + (a + 1) * BLK]

    for near in range(STEP):
        for m in range(3):
            code = code_ref[m, turn * STEP + near]
            where = jnp.maximum(code - 1, 0)
            feat = where // 64 * DB + where % 8
            hid = where % 64 // 8
            left, right = ((xt.at[feat], dg.at[hid]), (xt.at[feat], du.at[hid]), (ht.at[hid], dy.at[feat]))[m]
            value = jnp.dot(left[...], right[...], preferred_element_type=F32)
            out_ref[m, near] = jnp.where(code > 0, value, 0.0).astype(BF)


def body(activations, out_grad, gate_blocks, up_blocks, down_blocks, block_index, block_dest):
    row = lax.axis_index("row")
    col = lax.axis_index("col")
    group = row // QUARTERS
    quarter = row % QUARTERS
    place = jnp.stack([row % 2, row // 2 % 2 * 2 + col]).astype(jnp.int32)
    all_index = lax.dynamic_index_in_dim(block_index, col, axis=2, keepdims=False)
    own_index = lax.dynamic_index_in_dim(all_index, row, axis=1, keepdims=False)

    tie = lax.optimization_barrier
    shard = jnp.concatenate([activations, out_grad], axis=1)
    pair = jnp.concatenate([shard, row_swap(shard, Y_MASK)], axis=0)
    near = jnp.concatenate([pair] + [row_swap(pair, z_mask(i)) for i in range(1, 4)], axis=0)
    pieces = [near] + [row_swap(near, x_mask(i)) for i in range(1, 4)]
    mirror = row_swap(near, 2)

    wide = [sds((DQ, HB), BF), sds((DQ, HB), BF), sds((HB, DQ), BF)]
    wg, wu, wd = call(dense_kernel, wide, [SMEM] + [VMEM] * 3)(
        own_index,
        gate_blocks.reshape(CAP, BLK, BLK),
        up_blocks.reshape(CAP, BLK, BLK),
        down_blocks.reshape(CAP, BLK, BLK),
    )
    dest = lax.dynamic_slice_in_dim(block_dest[:, :, 0, :], group * QUARTERS, QUARTERS, axis=1)
    index = lax.dynamic_slice_in_dim(all_index, group * QUARTERS, QUARTERS, axis=1)
    swap = (jnp.arange(QUARTERS, dtype=jnp.int32) ^ quarter)[None, :, None]
    value = (swap * 64 + index + 1).reshape(3, 1, QUARTERS * CAP)
    targets = quarter * CAP + jnp.arange(CAP, dtype=jnp.int32)
    hits = dest.reshape(3, 1, QUARTERS * CAP) == targets[None, :, None]
    code = jnp.sum(jnp.where(hits, value, 0), axis=2, dtype=jnp.int32)
    pieces, mirror, code = tie((pieces, mirror, code))

    half = sds((128, 3 * HB), F32)
    keep, send = call(
        partial_kernel, [half, half], [SMEM] + [VMEM] * 7, scratch=[pltpu.VMEM((TOKENS, 2 * DQ), BF)]
    )(place, *pieces, wg, wu, wd)
    got = row_swap(send, 1)
    fours = call(pair_kernel, [sds((32, 3 * HB), F32)] * 4, [SMEM, VMEM, VMEM])(place, keep, got)
    sums = [fours[0]] + [square_swap(fours[i], i) for i in range(1, 4)]

    pieces, mirror, keep = tie((pieces, mirror, keep))
    mirrors = [mirror] + [row_swap(mirror, x_mask(i)) for i in range(1, 4)]
    prepped = [sds((DB, BLK, TOKENS), BF), sds((DB, TOKENS, BLK), BF)]
    prep = call(prep_kernel, prepped, [VMEM] * 4, scratch=[pltpu.VMEM((TOKENS, 2 * DQ), BF)])
    x0, y0 = prep(*pieces)
    sums, mirrors, x0, y0 = tie((sums, mirrors, x0, y0))

    share = call(act_kernel, sds((32, 3 * HB), BF), [VMEM] * 4)(*sums)
    mine = [share] + [square_swap(share, i) for i in range(1, 4)]
    x2, y2 = prep(*tie((mirrors, share))[0])
    x1, y1 = [row_swap(v, 1) for v in (x0, y0)]
    mine, x1, y1, x2, y2 = tie((mine, x1, y1, x2, y2))
    mine = jnp.concatenate(mine, axis=0)
    theirs = row_swap(mine, 1)
    outs = call(
        out_kernel,
        [sds((64, 2 * DQ), F32)] + [sds((64, 2 * DQ), BF)] * 3 + [sds((TOKENS, 3 * HB), BF)],
        [SMEM] + [VMEM] * 5,
    )(place, mine, theirs, wg, wu, wd)
    full = outs[4]
    x3, y3 = [row_swap(v, 1) for v in tie((x2, y2, mine))[:2]]
    far = [row_swap(outs[i], x_mask(i)) for i in range(1, 4)]

    grads = call(
        grad_kernel,
        sds((3, CAP, BLK, BLK), BF),
        [SMEM] + [VMEM] * 9,
        out_specs=pl.BlockSpec((3, STEP, BLK, BLK), lambda i: (0, i, 0, 0)),
        scratch=[
            pltpu.VMEM((QUARTERS * DB, BLK, TOKENS), BF),
            pltpu.VMEM((QUARTERS * DB, TOKENS, BLK), BF),
            pltpu.VMEM((FB, BLK, TOKENS), BF),
            pltpu.VMEM((FB, TOKENS, BLK), BF),
            pltpu.VMEM((FB, TOKENS, BLK), BF),
        ],
        grid=(CAP // STEP,),
        limit=24,
    )(code, full, x0, x1, x2, x3, y0, y1, y2, y3)
    far, grads = tie((far, grads))
    total = outs[0] + far[0].astype(F32) + far[1].astype(F32) + far[2].astype(F32)
    last = total[: 2 * TG]
    for i in range(1, 4):
        last = last + row_swap(total[i * 2 * TG : (i + 1) * 2 * TG].astype(BF), z_mask(i)).astype(F32)
    last = (last[:TG] + row_swap(last[TG:].astype(BF), Y_MASK).astype(F32)).astype(BF)
    return last[:, :DQ], last[:, DQ:], grads.reshape(3, 1, 1, CAP, BLK, BLK)


def solution(mesh):
    return jax.shard_map(
        body,
        mesh=mesh,
        in_specs=(
            P("row", "col"),
            P("row", "col"),
            P("row", "col", None, None, None),
            P("row", "col", None, None, None),
            P("row", "col", None, None, None),
            P(),
            P(None, None, "col", None),
        ),
        out_specs=(P("row", "col"), P("row", "col"), P(None, "row", "col", None, None, None)),
        check_vma=False,
    )
```

```python
import functools

import jax
import jax.numpy as jnp
from jax import lax
from jax.experimental import pallas as pl
from jax.experimental.pallas import tpu as pltpu
from jax.sharding import PartitionSpec as P

BLK = 128
QUARTERS = 4
FB = 7
DB = 8
SLOTS = 56
CAP = 48
DQ = 1024
HB = 896
TG = 8
STEP = 8
TOKENS = 256
BF = jnp.bfloat16
F32 = jnp.float32
NT = (((1,), (1,)), ((), ()))
VMEM = pl.BlockSpec(memory_space=pltpu.VMEM)
SMEM = pl.BlockSpec(memory_space=pltpu.SMEM)


def row_swap(value, mask):
    return lax.ppermute(value, "row", [(i, i ^ mask) for i in range(128)])


def square_swap(value, step):
    mask = (step >> 1) * 4 | (step & 1)
    return lax.ppermute(value, ("row", "col"), [(i, i ^ mask) for i in range(256)])


def z_mask(step):
    return step << 2


Y_MASK = 64


def x_mask(step):
    return step << 4


def sds(shape, dtype):
    return jax.ShapeDtypeStruct(shape, dtype)


def call(kernel, out_shape, in_specs, out_specs=None, scratch=(), limit=16, grid=()):
    many = isinstance(out_shape, (tuple, list))
    if out_specs is None:
        out_specs = [VMEM] * len(out_shape) if many else VMEM
    return pl.pallas_call(
        kernel,
        out_shape=out_shape,
        in_specs=in_specs,
        out_specs=out_specs,
        grid=grid,
        scratch_shapes=list(scratch),
        compiler_params=pltpu.CompilerParams(vmem_limit_bytes=limit * 2**20),
    )


def dense_kernel(index_ref, gate_ref, up_ref, down_ref, wg_ref, wu_ref, wd_ref):
    wg_ref[...] = jnp.zeros_like(wg_ref)
    wu_ref[...] = jnp.zeros_like(wu_ref)
    wd_ref[...] = jnp.zeros_like(wd_ref)

    def one(slot, carry):
        for m, (blocks, dense) in enumerate(((gate_ref, wg_ref), (up_ref, wu_ref), (down_ref, wd_ref))):
            place = index_ref[m, slot]

            @pl.when(place < SLOTS)
            def _():
                hid = pl.multiple_of(place // DB * BLK, BLK)
                feat = pl.multiple_of(place % DB * BLK, BLK)
                first, second = (hid, feat) if m == 2 else (feat, hid)
                dense[pl.ds(first, BLK), pl.ds(second, BLK)] = blocks[slot]

        return carry

    lax.fori_loop(0, CAP, one, 0)


def partial_kernel(place_ref, p0, p1, p2, p3, wg_ref, wu_ref, wd_ref, out_ref, rows, *, other):
    swap = place_ref[0] != other

    @pl.when(swap)
    def _():
        rows[:64, :] = p2[...]
        rows[64:, :] = p3[...]

    @pl.when(jnp.logical_not(swap))
    def _():
        rows[:64, :] = p0[...]
        rows[64:, :] = p1[...]

    x = rows[:, :DQ]
    dy = rows[:, DQ:]
    out_ref[:, :HB] = jnp.dot(x, wg_ref[...], preferred_element_type=F32)
    out_ref[:, HB : 2 * HB] = jnp.dot(x, wu_ref[...], preferred_element_type=F32)
    out_ref[:, 2 * HB :] = lax.dot_general(dy, wd_ref[...], NT, preferred_element_type=F32)


def pair_kernel(place_ref, keep_ref, got_ref, o0, o1, o2, o3):
    me = place_ref[1]
    lane = lax.broadcasted_iota(jnp.int32, (32, BLK), 1)
    for step, out in enumerate((o0, o1, o2, o3)):
        at = pl.ds(pl.multiple_of((me ^ step) * 32, 32), 32)
        if step == 0:
            out[...] = keep_ref[at, :] + got_ref[at, :]
            continue
        scales = jnp.zeros((32, BLK), F32)
        for m in range(3):
            part = slice(m * HB, (m + 1) * HB)
            value = keep_ref[at, part] + got_ref[at, part]
            top = jnp.max(jnp.abs(value), axis=1, keepdims=True)
            power = jnp.clip(jnp.ceil(jnp.log2(jnp.maximum(top, 1e-35))), -110.0, 120.0)
            whole = jnp.round(value * jnp.exp2(15.0 - power))
            out[:, part] = jnp.clip(whole, -32767.0, 32767.0).astype(jnp.int16)
            scales = jnp.where(lane >= m * 32, power, scales)
        out[:, 3 * HB :] = scales.astype(jnp.int16)


def act_kernel(a0, a1, a2, a3, out_ref):
    scales = [a[:, 3 * HB :].astype(F32) for a in (a1, a2, a3)]

    def total(m):
        part = slice(m * HB, (m + 1) * HB)
        value = a0[:, part]
        for a, scale in zip((a1, a2, a3), scales):
            value += a[:, part].astype(F32) * jnp.exp2(scale[:, m * 32 : m * 32 + 1] - 15.0)
        return value

    gate, up, dh = total(0), total(1), total(2)
    sig = jax.nn.sigmoid(gate)
    silu = gate * sig
    out_ref[:, :HB] = (silu * up).astype(BF)
    out_ref[:, HB : 2 * HB] = (dh * up * sig * (1.0 + gate * (1.0 - sig))).astype(BF)
    out_ref[:, 2 * HB :] = (dh * silu).astype(BF)


def spread(place_ref, mine, theirs, rows):
    core, me = place_ref[0], place_ref[1]
    for step in range(4):
        at = pl.multiple_of(core * 128 + (me ^ step) * 32, 32)
        rows[pl.ds(at, 32), :] = mine[step * 32 : (step + 1) * 32, :]
        at = pl.multiple_of((1 - core) * 128 + (me ^ step) * 32, 32)
        rows[pl.ds(at, 32), :] = theirs[step * 32 : (step + 1) * 32, :]


def out_kernel(place_ref, mine, theirs, wg_ref, wu_ref, wd_ref, t0, t1, t2, t3, full_ref):
    spread(place_ref, mine, theirs, full_ref)
    mixed = jnp.dot(full_ref[:, :HB], wd_ref[...], preferred_element_type=F32)
    for step, out in enumerate((t0, t1, t2, t3)):
        out[:, :DQ] = mixed[step * 64 : (step + 1) * 64].astype(out.dtype)
    grad = lax.dot_general(full_ref[:, HB : 2 * HB], wg_ref[...], NT, preferred_element_type=F32)
    grad += lax.dot_general(full_ref[:, 2 * HB :], wu_ref[...], NT, preferred_element_type=F32)
    for step, out in enumerate((t0, t1, t2, t3)):
        out[:, DQ:] = grad[step * 64 : (step + 1) * 64].astype(out.dtype)


def prep_kernel(p0, p1, p2, p3, out_ref):
    for b in range(DB):
        for side, pair in enumerate(((p0, p1), (p2, p3))):
            lanes = slice(side * 128, (side + 1) * 128)
            x = jnp.concatenate([p[:, b * BLK : (b + 1) * BLK] for p in pair], axis=0)
            out_ref[b, :, lanes] = x.T
            for low, p in enumerate(pair):
                out_ref[DB + b, low * 64 : (low + 1) * 64, lanes] = p[:, DQ + b * BLK : DQ + (b + 1) * BLK]


def grad_kernel(code_ref, full, s0, s1, s2, s3, out_ref, slab, ht, dg, du):
    turn = pl.program_id(0)

    @pl.when(turn == 0)
    def _():
        for j, source in enumerate((s0, s1, s2, s3)):
            slab[j * 2 * DB : (j + 1) * 2 * DB] = source[...]
        for a in range(FB):
            ht[a] = full[:, a * BLK : (a + 1) * BLK].T
            dg[a] = full[:, HB + a * BLK : HB + (a + 1) * BLK]
            du[a] = full[:, 2 * HB + a * BLK : 2 * HB + (a + 1) * BLK]

    for near in range(STEP):
        for m in range(3):
            code = code_ref[m, turn * STEP + near]
            where = jnp.maximum(code - 1, 0)
            feat = where // 64 * 2 * DB + where % 8
            hid = where % 64 // 8
            if m == 2:
                left = ht[hid]
                right = jnp.concatenate([slab[feat + DB, :, :128], slab[feat + DB, :, 128:]], axis=0)
            else:
                left = slab[feat]
                right = (dg, du)[m][hid]
            value = jnp.dot(left, right, preferred_element_type=F32)
            out_ref[m, near] = jnp.where(code > 0, value, 0.0).astype(BF)


def body(activations, out_grad, gate_blocks, up_blocks, down_blocks, block_index, block_dest):
    row = lax.axis_index("row")
    col = lax.axis_index("col")
    group = row // QUARTERS
    quarter = row % QUARTERS
    place = jnp.stack([row % 2, row // 2 % 2 * 2 + col]).astype(jnp.int32)
    all_index = lax.dynamic_index_in_dim(block_index, col, axis=2, keepdims=False)
    own_index = lax.dynamic_index_in_dim(all_index, row, axis=1, keepdims=False)

    tie = lax.optimization_barrier
    shard = jnp.concatenate([activations, out_grad], axis=1)
    pair = jnp.concatenate([shard, row_swap(shard, Y_MASK)], axis=0)
    near = jnp.concatenate([pair] + [row_swap(pair, z_mask(i)) for i in range(1, 4)], axis=0)
    pieces = [near] + [row_swap(near, x_mask(i)) for i in range(1, 4)]
    mirror = row_swap(near, 2)

    wide = [sds((DQ, HB), BF), sds((DQ, HB), BF), sds((HB, DQ), BF)]
    wg, wu, wd = call(dense_kernel, wide, [SMEM] + [VMEM] * 3)(
        own_index,
        gate_blocks.reshape(CAP, BLK, BLK),
        up_blocks.reshape(CAP, BLK, BLK),
        down_blocks.reshape(CAP, BLK, BLK),
    )
    dest = lax.dynamic_slice_in_dim(block_dest[:, :, 0, :], group * QUARTERS, QUARTERS, axis=1)
    index = lax.dynamic_slice_in_dim(all_index, group * QUARTERS, QUARTERS, axis=1)
    swap = (jnp.arange(QUARTERS, dtype=jnp.int32) ^ quarter)[None, :, None]
    value = (swap * 64 + index + 1).reshape(3, 1, QUARTERS * CAP)
    targets = quarter * CAP + jnp.arange(CAP, dtype=jnp.int32)
    hits = dest.reshape(3, 1, QUARTERS * CAP) == targets[None, :, None]
    code = jnp.sum(jnp.where(hits, value, 0), axis=2, dtype=jnp.int32)
    pieces, mirror, code = tie((pieces, mirror, code))

    half = sds((128, 3 * HB), F32)

    def partial(other):
        return call(
            functools.partial(partial_kernel, other=other),
            half,
            [SMEM] + [VMEM] * 7,
            scratch=[pltpu.VMEM((128, 2 * DQ), BF)],
        )(place, *pieces, wg, wu, wd)

    send = partial(1)
    got = row_swap(send, 1)
    keep = partial(0)
    coded = sds((32, 3 * HB + BLK), jnp.int16)
    sums = call(pair_kernel, [sds((32, 3 * HB), F32)] + [coded] * 3, [SMEM, VMEM, VMEM])(place, keep, got)
    sums = [sums[0]] + [square_swap(sums[i], i) for i in range(1, 4)]

    pieces, mirror, keep = tie((pieces, mirror, keep))
    mirror1, mirror3 = row_swap(mirror, x_mask(1)), row_swap(mirror, x_mask(3))
    prep = call(prep_kernel, sds((2 * DB, BLK, TOKENS), BF), [VMEM] * 4)
    slab0 = prep(*pieces)
    sums, mirror1, mirror3, slab0 = tie((sums, mirror1, mirror3, slab0))

    share = call(act_kernel, sds((32, 3 * HB), BF), [VMEM] * 4)(*sums)
    mine = [share] + [square_swap(share, i) for i in range(1, 4)]
    mirror, slab0, share = tie((mirror, slab0, share))
    mirror2 = row_swap(mirror, x_mask(2))
    slab1 = row_swap(slab0, 1)
    mine, mirror2, slab1 = tie((mine, mirror2, slab1))

    mine = jnp.concatenate(mine, axis=0)
    theirs = row_swap(mine, 1)
    slab2 = prep(mirror, mirror1, mirror2, mirror3)
    theirs, slab2 = tie((theirs, slab2))
    outs = call(
        out_kernel,
        [sds((64, 2 * DQ), F32)] + [sds((64, 2 * DQ), BF)] * 3 + [sds((TOKENS, 3 * HB), BF)],
        [SMEM] + [VMEM] * 5,
    )(place, mine, theirs, wg, wu, wd)
    full = outs[4]
    slab2, full = tie((slab2, full))
    slab3 = row_swap(slab2, 1)
    far1, far2, far3 = [row_swap(outs[i], x_mask(i)) for i in range(1, 4)]

    grads = call(
        grad_kernel,
        sds((3, CAP, BLK, BLK), BF),
        [SMEM] + [VMEM] * 5,
        out_specs=pl.BlockSpec((3, STEP, BLK, BLK), lambda i: (0, i, 0, 0)),
        scratch=[
            pltpu.VMEM((QUARTERS * 2 * DB, BLK, TOKENS), BF),
            pltpu.VMEM((FB, BLK, TOKENS), BF),
            pltpu.VMEM((FB, TOKENS, BLK), BF),
            pltpu.VMEM((FB, TOKENS, BLK), BF),
        ],
        grid=(CAP // STEP,),
        limit=24,
    )(code, full, slab0, slab1, slab2, slab3)
    far1, far2, far3, grads = tie((far1, far2, far3, grads))
    total = outs[0] + far1.astype(F32) + far2.astype(F32) + far3.astype(F32)
    last = total[: 2 * TG]
    for i in range(1, 4):
        last = last + row_swap(total[i * 2 * TG : (i + 1) * 2 * TG].astype(BF), z_mask(i)).astype(F32)
    last = (last[:TG] + row_swap(last[TG:].astype(BF), Y_MASK).astype(F32)).astype(BF)
    return last[:, :DQ], last[:, DQ:], grads.reshape(3, 1, 1, CAP, BLK, BLK)


def solution(mesh):
    return jax.shard_map(
        body,
        mesh=mesh,
        in_specs=(
            P("row", "col"),
            P("row", "col"),
            P("row", "col", None, None, None),
            P("row", "col", None, None, None),
            P("row", "col", None, None, None),
            P(),
            P(None, None, "col", None),
        ),
        out_specs=(P("row", "col"), P("row", "col"), P(None, "row", "col", None, None, None)),
        check_vma=False,
    )
```

```python
import functools

import jax
import jax.numpy as jnp
from jax import lax
from jax.experimental import pallas as pl
from jax.experimental.pallas import tpu as pltpu
from jax.sharding import PartitionSpec as P

BLK = 128
QUARTERS = 4
FB = 7
DB = 8
SLOTS = 56
CAP = 48
DQ = 1024
HB = 896
TG = 8
STEP = 8
TOKENS = 256
BF = jnp.bfloat16
F32 = jnp.float32
NT = (((1,), (1,)), ((), ()))
VMEM = pl.BlockSpec(memory_space=pltpu.VMEM)
SMEM = pl.BlockSpec(memory_space=pltpu.SMEM)


def row_swap(value, mask):
    return lax.ppermute(value, "row", [(i, i ^ mask) for i in range(128)])


def square_swap(value, step):
    mask = (step >> 1) * 4 | (step & 1)
    return lax.ppermute(value, ("row", "col"), [(i, i ^ mask) for i in range(256)])


def z_mask(step):
    return step << 2


Y_MASK = 64


def x_mask(step):
    return step << 4


def sds(shape, dtype):
    return jax.ShapeDtypeStruct(shape, dtype)


def call(kernel, out_shape, in_specs, out_specs=None, scratch=(), limit=16, grid=()):
    many = isinstance(out_shape, (tuple, list))
    if out_specs is None:
        out_specs = [VMEM] * len(out_shape) if many else VMEM
    return pl.pallas_call(
        kernel,
        out_shape=out_shape,
        in_specs=in_specs,
        out_specs=out_specs,
        grid=grid,
        scratch_shapes=list(scratch),
        compiler_params=pltpu.CompilerParams(vmem_limit_bytes=limit * 2**20),
    )


def dense_kernel(index_ref, gate_ref, up_ref, down_ref, wg_ref, wu_ref, wd_ref):
    wg_ref[...] = jnp.zeros_like(wg_ref)
    wu_ref[...] = jnp.zeros_like(wu_ref)
    wd_ref[...] = jnp.zeros_like(wd_ref)

    def one(slot, carry):
        for m, (blocks, dense) in enumerate(((gate_ref, wg_ref), (up_ref, wu_ref), (down_ref, wd_ref))):
            place = index_ref[m, slot]

            @pl.when(place < SLOTS)
            def _():
                hid = pl.multiple_of(place // DB * BLK, BLK)
                feat = pl.multiple_of(place % DB * BLK, BLK)
                first, second = (hid, feat) if m == 2 else (feat, hid)
                dense[pl.ds(first, BLK), pl.ds(second, BLK)] = blocks[slot]

        return carry

    lax.fori_loop(0, CAP, one, 0)


def partial_kernel(place_ref, p0, p1, p2, p3, wg_ref, wu_ref, wd_ref, out_ref, rows, *, other):
    swap = place_ref[0] != other

    @pl.when(swap)
    def _():
        rows[:64, :] = p2[...]
        rows[64:, :] = p3[...]

    @pl.when(jnp.logical_not(swap))
    def _():
        rows[:64, :] = p0[...]
        rows[64:, :] = p1[...]

    x = rows[:, :DQ]
    dy = rows[:, DQ:]
    out_ref[:, :HB] = jnp.dot(x, wg_ref[...], preferred_element_type=F32)
    out_ref[:, HB : 2 * HB] = jnp.dot(x, wu_ref[...], preferred_element_type=F32)
    out_ref[:, 2 * HB :] = lax.dot_general(dy, wd_ref[...], NT, preferred_element_type=F32)


def pair_kernel(place_ref, keep_ref, got_ref, o0, o1, o2, o3):
    me = place_ref[1]
    lane = lax.broadcasted_iota(jnp.int32, (32, BLK), 1)
    for step, out in enumerate((o0, o1, o2, o3)):
        at = pl.ds(pl.multiple_of((me ^ step) * 32, 32), 32)
        if step == 0:
            out[...] = keep_ref[at, :] + got_ref[at, :]
            continue
        scales = jnp.zeros((32, BLK), F32)
        for m in range(3):
            part = slice(m * HB, (m + 1) * HB)
            value = keep_ref[at, part] + got_ref[at, part]
            top = jnp.max(jnp.abs(value), axis=1, keepdims=True)
            power = jnp.clip(jnp.ceil(jnp.log2(jnp.maximum(top, 1e-35))), -110.0, 120.0)
            whole = jnp.round(value * jnp.exp2(15.0 - power))
            out[:, part] = jnp.clip(whole, -32767.0, 32767.0).astype(jnp.int16)
            scales = jnp.where(lane >= m * 32, power, scales)
        out[:, 3 * HB :] = scales.astype(jnp.int16)


def act_kernel(a0, a1, a2, a3, out_ref):
    scales = [a[:, 3 * HB :].astype(F32) for a in (a1, a2, a3)]

    def total(m):
        part = slice(m * HB, (m + 1) * HB)
        value = a0[:, part]
        for a, scale in zip((a1, a2, a3), scales):
            value += a[:, part].astype(F32) * jnp.exp2(scale[:, m * 32 : m * 32 + 1] - 15.0)
        return value

    gate, up, dh = total(0), total(1), total(2)
    sig = jax.nn.sigmoid(gate)
    silu = gate * sig
    out_ref[:, :HB] = (silu * up).astype(BF)
    out_ref[:, HB : 2 * HB] = (dh * up * sig * (1.0 + gate * (1.0 - sig))).astype(BF)
    out_ref[:, 2 * HB :] = (dh * silu).astype(BF)


def spread(place_ref, mine, theirs, rows):
    core, me = place_ref[0], place_ref[1]
    for step in range(4):
        at = pl.multiple_of(core * 128 + (me ^ step) * 32, 32)
        rows[pl.ds(at, 32), :] = mine[step * 32 : (step + 1) * 32, :]
        at = pl.multiple_of((1 - core) * 128 + (me ^ step) * 32, 32)
        rows[pl.ds(at, 32), :] = theirs[step * 32 : (step + 1) * 32, :]


def out_kernel(place_ref, mine, theirs, wg_ref, wu_ref, wd_ref, t0, t1, t2, t3, full_ref):
    spread(place_ref, mine, theirs, full_ref)
    mixed = jnp.dot(full_ref[:, :HB], wd_ref[...], preferred_element_type=F32)
    for step, out in enumerate((t0, t1, t2, t3)):
        out[:, :DQ] = mixed[step * 64 : (step + 1) * 64].astype(out.dtype)
    grad = lax.dot_general(full_ref[:, HB : 2 * HB], wg_ref[...], NT, preferred_element_type=F32)
    grad += lax.dot_general(full_ref[:, 2 * HB :], wu_ref[...], NT, preferred_element_type=F32)
    for step, out in enumerate((t0, t1, t2, t3)):
        out[:, DQ:] = grad[step * 64 : (step + 1) * 64].astype(out.dtype)


def prep_kernel(p0, p1, p2, p3, out_ref):
    for b in range(DB):
        for side, pair in enumerate(((p0, p1), (p2, p3))):
            lanes = slice(side * 128, (side + 1) * 128)
            x = jnp.concatenate([p[:, b * BLK : (b + 1) * BLK] for p in pair], axis=0)
            out_ref[b, :, lanes] = x.T
            for low, p in enumerate(pair):
                out_ref[DB + b, low * 64 : (low + 1) * 64, lanes] = p[:, DQ + b * BLK : DQ + (b + 1) * BLK]


def grad_kernel(code_ref, full, s0, s1, s2, s3, out_ref, slab, ht, dg, du):
    turn = pl.program_id(0)

    @pl.when(turn == 0)
    def _():
        for j, source in enumerate((s0, s1, s2, s3)):
            slab[j * 2 * DB : (j + 1) * 2 * DB] = source[...]
        for a in range(FB):
            ht[a] = full[:, a * BLK : (a + 1) * BLK].T
            dg[a] = full[:, HB + a * BLK : HB + (a + 1) * BLK]
            du[a] = full[:, 2 * HB + a * BLK : 2 * HB + (a + 1) * BLK]

    for near in range(STEP):
        for m in range(3):
            code = code_ref[m, turn * STEP + near]
            where = jnp.maximum(code - 1, 0)
            feat = where // 64 * 2 * DB + where % 8
            hid = where % 64 // 8
            if m == 2:
                left = ht[hid]
                right = jnp.concatenate([slab[feat + DB, :, :128], slab[feat + DB, :, 128:]], axis=0)
            else:
                left = slab[feat]
                right = (dg, du)[m][hid]
            value = jnp.dot(left, right, preferred_element_type=F32)
            out_ref[m, near] = jnp.where(code > 0, value, 0.0).astype(BF)


def body(activations, out_grad, gate_blocks, up_blocks, down_blocks, block_index, block_dest):
    row = lax.axis_index("row")
    col = lax.axis_index("col")
    group = row // QUARTERS
    quarter = row % QUARTERS
    place = jnp.stack([row % 2, row // 2 % 2 * 2 + col]).astype(jnp.int32)
    all_index = lax.dynamic_index_in_dim(block_index, col, axis=2, keepdims=False)
    own_index = lax.dynamic_index_in_dim(all_index, row, axis=1, keepdims=False)

    tie = lax.optimization_barrier
    other = [row_swap(activations, Y_MASK), row_swap(out_grad, Y_MASK)]
    pair = jnp.concatenate(
        [jnp.concatenate([activations, out_grad], axis=1), jnp.concatenate(other, axis=1)], axis=0
    )
    near = jnp.concatenate([pair] + [row_swap(pair, z_mask(i)) for i in range(1, 4)], axis=0)
    pieces = [near] + [row_swap(near, x_mask(i)) for i in range(1, 4)]
    mirror = row_swap(near, 2)

    wide = [sds((DQ, HB), BF), sds((DQ, HB), BF), sds((HB, DQ), BF)]
    wg, wu, wd = call(dense_kernel, wide, [SMEM] + [VMEM] * 3)(
        own_index,
        gate_blocks.reshape(CAP, BLK, BLK),
        up_blocks.reshape(CAP, BLK, BLK),
        down_blocks.reshape(CAP, BLK, BLK),
    )
    dest = lax.dynamic_slice_in_dim(block_dest[:, :, 0, :], group * QUARTERS, QUARTERS, axis=1)
    index = lax.dynamic_slice_in_dim(all_index, group * QUARTERS, QUARTERS, axis=1)
    swap = (jnp.arange(QUARTERS, dtype=jnp.int32) ^ quarter)[None, :, None]
    value = (swap * 64 + index + 1).reshape(3, 1, QUARTERS * CAP)
    targets = quarter * CAP + jnp.arange(CAP, dtype=jnp.int32)
    hits = dest.reshape(3, 1, QUARTERS * CAP) == targets[None, :, None]
    code = jnp.sum(jnp.where(hits, value, 0), axis=2, dtype=jnp.int32)
    pieces, mirror, code = tie((pieces, mirror, code))

    half = sds((128, 3 * HB), F32)

    def partial(other):
        return call(
            functools.partial(partial_kernel, other=other),
            half,
            [SMEM] + [VMEM] * 7,
            scratch=[pltpu.VMEM((128, 2 * DQ), BF)],
        )(place, *pieces, wg, wu, wd)

    send = partial(1)
    got = row_swap(send, 1)
    keep = partial(0)
    coded = sds((32, 3 * HB + BLK), jnp.int16)
    sums = call(pair_kernel, [sds((32, 3 * HB), F32)] + [coded] * 3, [SMEM, VMEM, VMEM])(place, keep, got)
    sums = [sums[0]] + [square_swap(sums[i], i) for i in range(1, 4)]

    prep = call(prep_kernel, sds((2 * DB, BLK, TOKENS), BF), [VMEM] * 4)
    mirror, keep = tie((mirror, keep))
    mirror1, mirror2, mirror3 = [row_swap(mirror, x_mask(i)) for i in (1, 2, 3)]
    slab0 = prep(*tie((pieces, sums[0]))[0])
    sums, mirror1, slab0 = tie((sums, mirror1, slab0))
    share = call(act_kernel, sds((32, 3 * HB), BF), [VMEM] * 4)(*sums)
    mine = [share] + [square_swap(share, i) for i in range(1, 4)]
    slab1 = row_swap(slab0, 1)
    mine, mirror2, mirror3 = tie((mine, mirror2, mirror3))
    mine = jnp.concatenate(mine, axis=0)
    theirs = row_swap(mine, 1)
    slab2 = prep(mirror, mirror1, mirror2, mirror3)
    theirs, slab2, slab1 = tie((theirs, slab2, slab1))
    outs = call(
        out_kernel,
        [sds((64, 2 * DQ), F32)] + [sds((64, 2 * DQ), BF)] * 3 + [sds((TOKENS, 3 * HB), BF)],
        [SMEM] + [VMEM] * 5,
    )(place, mine, theirs, wg, wu, wd)
    full = outs[4]
    slab2, full = tie((slab2, full))
    slab3 = row_swap(slab2, 1)
    far1, far2, far3 = [row_swap(outs[i], x_mask(i)) for i in range(1, 4)]

    grads = call(
        grad_kernel,
        sds((3, CAP, BLK, BLK), BF),
        [SMEM] + [VMEM] * 5,
        out_specs=pl.BlockSpec((3, STEP, BLK, BLK), lambda i: (0, i, 0, 0)),
        scratch=[
            pltpu.VMEM((QUARTERS * 2 * DB, BLK, TOKENS), BF),
            pltpu.VMEM((FB, BLK, TOKENS), BF),
            pltpu.VMEM((FB, TOKENS, BLK), BF),
            pltpu.VMEM((FB, TOKENS, BLK), BF),
        ],
        grid=(CAP // STEP,),
        limit=24,
    )(code, full, slab0, slab1, slab2, slab3)
    far1, far2, far3, grads = tie((far1, far2, far3, grads))
    total = outs[0] + far1.astype(F32) + far2.astype(F32) + far3.astype(F32)
    last = total[: 2 * TG]
    for i in range(1, 4):
        last = last + row_swap(total[i * 2 * TG : (i + 1) * 2 * TG].astype(BF), z_mask(i)).astype(F32)
    got = row_swap(last[TG:].astype(BF), Y_MASK).astype(F32)
    mixed_rows, input_grad = [(last[:TG, c] + got[:, c]).astype(BF) for c in (slice(0, DQ), slice(DQ, 2 * DQ))]
    return mixed_rows, input_grad, grads.reshape(3, 1, 1, CAP, BLK, BLK)


def solution(mesh):
    return jax.shard_map(
        body,
        mesh=mesh,
        in_specs=(
            P("row", "col"),
            P("row", "col"),
            P("row", "col", None, None, None),
            P("row", "col", None, None, None),
            P("row", "col", None, None, None),
            P(),
            P(None, None, "col", None),
        ),
        out_specs=(P("row", "col"), P("row", "col"), P(None, "row", "col", None, None, None)),
        check_vma=False,
    )
```

```python
import functools

import jax
import jax.numpy as jnp
from jax import lax
from jax.experimental import pallas as pl
from jax.experimental.pallas import tpu as pltpu
from jax.sharding import PartitionSpec as P

BLK = 128
QUARTERS = 4
FB = 7
DB = 8
SLOTS = 56
CAP = 48
DQ = 1024
HB = 896
TG = 8
STEP = 8
TOKENS = 256
ORDER = (1, 3, 2)
BF = jnp.bfloat16
F32 = jnp.float32
NT = (((1,), (1,)), ((), ()))
VMEM = pl.BlockSpec(memory_space=pltpu.VMEM)
SMEM = pl.BlockSpec(memory_space=pltpu.SMEM)


def row_swap(value, mask):
    return lax.ppermute(value, "row", [(i, i ^ mask) for i in range(128)])


def square_swap(value, step):
    mask = (step >> 1) * 4 | (step & 1)
    return lax.ppermute(value, ("row", "col"), [(i, i ^ mask) for i in range(256)])


def z_mask(step):
    return step << 2


Y_MASK = 64


def x_mask(step):
    return step << 4


def sds(shape, dtype):
    return jax.ShapeDtypeStruct(shape, dtype)


def call(kernel, out_shape, in_specs, out_specs=None, scratch=(), limit=16, grid=()):
    many = isinstance(out_shape, (tuple, list))
    if out_specs is None:
        out_specs = [VMEM] * len(out_shape) if many else VMEM
    return pl.pallas_call(
        kernel,
        out_shape=out_shape,
        in_specs=in_specs,
        out_specs=out_specs,
        grid=grid,
        scratch_shapes=list(scratch),
        compiler_params=pltpu.CompilerParams(vmem_limit_bytes=limit * 2**20),
    )


def stack_kernel(p0, p1, p2, p3, out_ref):
    height = p0.shape[0]
    for at, piece in enumerate((p0, p1, p2, p3)):
        out_ref[at * height : (at + 1) * height, :] = piece[...]


def stack(parts):
    shape = (4 * parts[0].shape[0],) + parts[0].shape[1:]
    return call(stack_kernel, sds(shape, parts[0].dtype), [VMEM] * 4)(*parts)


def dense_kernel(index_ref, gate_ref, up_ref, down_ref, wg_ref, wu_ref, wd_ref):
    wg_ref[...] = jnp.zeros_like(wg_ref)
    wu_ref[...] = jnp.zeros_like(wu_ref)
    wd_ref[...] = jnp.zeros_like(wd_ref)

    def one(slot, carry):
        for m, (blocks, dense) in enumerate(((gate_ref, wg_ref), (up_ref, wu_ref), (down_ref, wd_ref))):
            place = index_ref[m, slot]

            @pl.when(place < SLOTS)
            def _():
                hid = pl.multiple_of(place // DB * BLK, BLK)
                feat = pl.multiple_of(place % DB * BLK, BLK)
                first, second = (hid, feat) if m == 2 else (feat, hid)
                dense[pl.ds(first, BLK), pl.ds(second, BLK)] = blocks[slot]

        return carry

    lax.fori_loop(0, CAP, one, 0)


def partial_kernel(place_ref, p0, p1, p2, p3, wg_ref, wu_ref, wd_ref, out_ref, rows, *, other):
    swap = place_ref[0] != other

    @pl.when(swap)
    def _():
        rows[:64, :] = p2[...]
        rows[64:, :] = p3[...]

    @pl.when(jnp.logical_not(swap))
    def _():
        rows[:64, :] = p0[...]
        rows[64:, :] = p1[...]

    x = rows[:, :DQ]
    dy = rows[:, DQ:]
    out_ref[:, :HB] = jnp.dot(x, wg_ref[...], preferred_element_type=F32)
    out_ref[:, HB : 2 * HB] = jnp.dot(x, wu_ref[...], preferred_element_type=F32)
    out_ref[:, 2 * HB :] = lax.dot_general(dy, wd_ref[...], NT, preferred_element_type=F32)


def pair_kernel(place_ref, keep_ref, got_ref, o0, o1, o2, o3):
    me = place_ref[1]
    lane = lax.broadcasted_iota(jnp.int32, (32, BLK), 1)
    for step, out in enumerate((o0, o1, o2, o3)):
        at = pl.ds(pl.multiple_of((me ^ step) * 32, 32), 32)
        if step == 0:
            out[...] = keep_ref[at, :] + got_ref[at, :]
            continue
        scales = jnp.zeros((32, BLK), F32)
        for m in range(3):
            part = slice(m * HB, (m + 1) * HB)
            value = keep_ref[at, part] + got_ref[at, part]
            top = jnp.max(jnp.abs(value), axis=1, keepdims=True)
            power = jnp.clip(jnp.ceil(jnp.log2(jnp.maximum(top, 1e-35))), -110.0, 120.0)
            whole = jnp.round(value * jnp.exp2(15.0 - power))
            out[:, part] = jnp.clip(whole, -32767.0, 32767.0).astype(jnp.int16)
            scales = jnp.where(lane >= m * 32, power, scales)
        out[:, 3 * HB :] = scales.astype(jnp.int16)


def act_kernel(a0, a1, a2, a3, out_ref):
    scales = [a[:, 3 * HB :].astype(F32) for a in (a1, a2, a3)]

    def total(m):
        part = slice(m * HB, (m + 1) * HB)
        value = a0[:, part]
        for a, scale in zip((a1, a2, a3), scales):
            value += a[:, part].astype(F32) * jnp.exp2(scale[:, m * 32 : m * 32 + 1] - 15.0)
        return value

    gate, up, dh = total(0), total(1), total(2)
    sig = jax.nn.sigmoid(gate)
    silu = gate * sig
    out_ref[:, :HB] = (silu * up).astype(BF)
    out_ref[:, HB : 2 * HB] = (dh * up * sig * (1.0 + gate * (1.0 - sig))).astype(BF)
    out_ref[:, 2 * HB :] = (dh * silu).astype(BF)


def spread(place_ref, mine, theirs, rows):
    core, me = place_ref[0], place_ref[1]
    for step in range(4):
        at = pl.multiple_of(core * 128 + (me ^ step) * 32, 32)
        rows[pl.ds(at, 32), :] = mine[step * 32 : (step + 1) * 32, :]
        at = pl.multiple_of((1 - core) * 128 + (me ^ step) * 32, 32)
        rows[pl.ds(at, 32), :] = theirs[step * 32 : (step + 1) * 32, :]


def out_kernel(place_ref, mine, theirs, wg_ref, wu_ref, wd_ref, t0, t1, t2, t3, full_ref):
    spread(place_ref, mine, theirs, full_ref)
    mixed = jnp.dot(full_ref[:, :HB], wd_ref[...], preferred_element_type=F32)
    for step, out in enumerate((t0, t1, t2, t3)):
        out[:, :DQ] = mixed[step * 64 : (step + 1) * 64].astype(out.dtype)
    grad = lax.dot_general(full_ref[:, HB : 2 * HB], wg_ref[...], NT, preferred_element_type=F32)
    grad += lax.dot_general(full_ref[:, 2 * HB :], wu_ref[...], NT, preferred_element_type=F32)
    for step, out in enumerate((t0, t1, t2, t3)):
        out[:, DQ:] = grad[step * 64 : (step + 1) * 64].astype(out.dtype)


def prep_kernel(p0, p1, p2, p3, out_ref):
    for b in range(DB):
        for side, pair in enumerate(((p0, p1), (p2, p3))):
            lanes = slice(side * 128, (side + 1) * 128)
            x = jnp.concatenate([p[:, b * BLK : (b + 1) * BLK] for p in pair], axis=0)
            out_ref[b, :, lanes] = x.T
            for low, p in enumerate(pair):
                out_ref[DB + b, low * 64 : (low + 1) * 64, lanes] = p[:, DQ + b * BLK : DQ + (b + 1) * BLK]


def grad_kernel(code_ref, full, s0, s1, s2, s3, out_ref, slab, ht, dg, du):
    turn = pl.program_id(0)

    @pl.when(turn == 0)
    def _():
        for j, source in enumerate((s0, s1, s2, s3)):
            slab[j * 2 * DB : (j + 1) * 2 * DB] = source[...]
        for a in range(FB):
            ht[a] = full[:, a * BLK : (a + 1) * BLK].T
            dg[a] = full[:, HB + a * BLK : HB + (a + 1) * BLK]
            du[a] = full[:, 2 * HB + a * BLK : 2 * HB + (a + 1) * BLK]

    for near in range(STEP):
        for m in range(3):
            code = code_ref[m, turn * STEP + near]
            where = jnp.maximum(code - 1, 0)
            feat = where // 64 * 2 * DB + where % 8
            hid = where % 64 // 8
            if m == 2:
                left = ht[hid]
                right = jnp.concatenate([slab[feat + DB, :, :128], slab[feat + DB, :, 128:]], axis=0)
            else:
                left = slab[feat]
                right = (dg, du)[m][hid]
            value = jnp.dot(left, right, preferred_element_type=F32)
            out_ref[m, near] = jnp.where(code > 0, value, 0.0).astype(BF)


def body(activations, out_grad, gate_blocks, up_blocks, down_blocks, block_index, block_dest):
    row = lax.axis_index("row")
    col = lax.axis_index("col")
    group = row // QUARTERS
    quarter = row % QUARTERS
    place = jnp.stack([row % 2, row // 2 % 2 * 2 + col]).astype(jnp.int32)
    all_index = lax.dynamic_index_in_dim(block_index, col, axis=2, keepdims=False)
    own_index = lax.dynamic_index_in_dim(all_index, row, axis=1, keepdims=False)

    tie = lax.optimization_barrier
    other = [row_swap(activations, Y_MASK), row_swap(out_grad, Y_MASK)]
    pair = jnp.concatenate(
        [jnp.concatenate([activations, out_grad], axis=1), jnp.concatenate(other, axis=1)], axis=0
    )
    near = stack([pair] + [row_swap(pair, z_mask(i)) for i in ORDER])
    pieces = [near] + [row_swap(near, x_mask(i)) for i in ORDER]
    mirror = row_swap(near, 2)

    wide = [sds((DQ, HB), BF), sds((DQ, HB), BF), sds((HB, DQ), BF)]
    wg, wu, wd = call(dense_kernel, wide, [SMEM] + [VMEM] * 3)(
        own_index,
        gate_blocks.reshape(CAP, BLK, BLK),
        up_blocks.reshape(CAP, BLK, BLK),
        down_blocks.reshape(CAP, BLK, BLK),
    )
    dest = lax.dynamic_slice_in_dim(block_dest[:, :, 0, :], group * QUARTERS, QUARTERS, axis=1)
    index = lax.dynamic_slice_in_dim(all_index, group * QUARTERS, QUARTERS, axis=1)
    swap = (jnp.arange(QUARTERS, dtype=jnp.int32) ^ quarter)[None, :, None]
    value = (swap * 64 + index + 1).reshape(3, 1, QUARTERS * CAP)
    targets = quarter * CAP + jnp.arange(CAP, dtype=jnp.int32)
    hits = dest.reshape(3, 1, QUARTERS * CAP) == targets[None, :, None]
    code = jnp.sum(jnp.where(hits, value, 0), axis=2, dtype=jnp.int32)
    pieces, mirror, code = tie((pieces, mirror, code))

    half = sds((128, 3 * HB), F32)

    def partial(other):
        return call(
            functools.partial(partial_kernel, other=other),
            half,
            [SMEM] + [VMEM] * 7,
            scratch=[pltpu.VMEM((128, 2 * DQ), BF)],
        )(place, *pieces, wg, wu, wd)

    send = partial(1)
    got = row_swap(send, 1)
    keep = partial(0)
    coded = sds((32, 3 * HB + BLK), jnp.int16)
    sums = call(pair_kernel, [sds((32, 3 * HB), F32)] + [coded] * 3, [SMEM, VMEM, VMEM])(place, keep, got)
    sums = [sums[0]] + [square_swap(sums[i], i) for i in (3, 1, 2)]

    prep = call(prep_kernel, sds((2 * DB, BLK, TOKENS), BF), [VMEM] * 4)
    mirror, keep = tie((mirror, keep))
    mirror1, mirror2, mirror3 = [row_swap(mirror, x_mask(i)) for i in ORDER]
    slab0 = prep(*tie((pieces, sums[0]))[0])
    sums, mirror1, slab0 = tie((sums, mirror1, slab0))
    share = call(act_kernel, sds((32, 3 * HB), BF), [VMEM] * 4)(*sums)
    mine = [share] + [square_swap(share, i) for i in range(1, 4)]
    slab1 = row_swap(slab0, 1)
    mine, mirror2, mirror3 = tie((mine, mirror2, mirror3))
    mine = jnp.concatenate(mine, axis=0)
    theirs = row_swap(mine, 1)
    slab2 = prep(mirror, mirror1, mirror2, mirror3)
    theirs, slab2, slab1 = tie((theirs, slab2, slab1))
    outs = call(
        out_kernel,
        [sds((64, 2 * DQ), F32)] + [sds((64, 2 * DQ), BF)] * 3 + [sds((TOKENS, 3 * HB), BF)],
        [SMEM] + [VMEM] * 5,
    )(place, mine, theirs, wg, wu, wd)
    full = outs[4]
    slab2, full = tie((slab2, full))
    slab3 = row_swap(slab2, 1)
    far3, far1, far2 = [row_swap(outs[at], x_mask(ORDER[at - 1])) for at in (3, 1, 2)]

    grads = call(
        grad_kernel,
        sds((3, CAP, BLK, BLK), BF),
        [SMEM] + [VMEM] * 5,
        out_specs=pl.BlockSpec((3, STEP, BLK, BLK), lambda i: (0, i, 0, 0)),
        scratch=[
            pltpu.VMEM((QUARTERS * 2 * DB, BLK, TOKENS), BF),
            pltpu.VMEM((FB, BLK, TOKENS), BF),
            pltpu.VMEM((FB, TOKENS, BLK), BF),
            pltpu.VMEM((FB, TOKENS, BLK), BF),
        ],
        grid=(CAP // STEP,),
        limit=24,
    )(code, full, slab0, slab1, slab2, slab3)
    far3, far1, far2, grads = tie((far3, far1, far2, grads))
    total = outs[0] + far3.astype(F32) + far1.astype(F32) + far2.astype(F32)
    last = total[: 2 * TG]
    for at in (3, 1, 2):
        part = total[at * 2 * TG : (at + 1) * 2 * TG].astype(BF)
        last = last + row_swap(part, z_mask(ORDER[at - 1])).astype(F32)
    got = row_swap(last[TG:].astype(BF), Y_MASK).astype(F32)
    mixed_rows, input_grad = [(last[:TG, c] + got[:, c]).astype(BF) for c in (slice(0, DQ), slice(DQ, 2 * DQ))]
    return mixed_rows, input_grad, grads.reshape(3, 1, 1, CAP, BLK, BLK)


def solution(mesh):
    return jax.shard_map(
        body,
        mesh=mesh,
        in_specs=(
            P("row", "col"),
            P("row", "col"),
            P("row", "col", None, None, None),
            P("row", "col", None, None, None),
            P("row", "col", None, None, None),
            P(),
            P(None, None, "col", None),
        ),
        out_specs=(P("row", "col"), P("row", "col"), P(None, "row", "col", None, None, None)),
        check_vma=False,
    )
```

```python
import functools

import jax
import jax.numpy as jnp
from jax import lax
from jax.experimental import pallas as pl
from jax.experimental.pallas import tpu as pltpu
from jax.sharding import PartitionSpec as P

BLK = 128
QUARTERS = 4
FB = 7
DB = 8
SLOTS = 56
CAP = 48
DQ = 1024
HB = 896
TG = 8
STEP = 8
TOKENS = 256
ORDER = (1, 3, 2)
BF = jnp.bfloat16
F32 = jnp.float32
NT = (((1,), (1,)), ((), ()))
VMEM = pl.BlockSpec(memory_space=pltpu.VMEM)
SMEM = pl.BlockSpec(memory_space=pltpu.SMEM)


def row_swap(value, mask):
    return lax.ppermute(value, "row", [(i, i ^ mask) for i in range(128)])


def square_swap(value, step):
    mask = (step >> 1) * 4 | (step & 1)
    return lax.ppermute(value, ("row", "col"), [(i, i ^ mask) for i in range(256)])


def z_mask(step):
    return step << 2


Y_MASK = 64


def x_mask(step):
    return step << 4


def sds(shape, dtype):
    return jax.ShapeDtypeStruct(shape, dtype)


def call(kernel, out_shape, in_specs, out_specs=None, scratch=(), limit=16, grid=()):
    many = isinstance(out_shape, (tuple, list))
    if out_specs is None:
        out_specs = [VMEM] * len(out_shape) if many else VMEM
    return pl.pallas_call(
        kernel,
        out_shape=out_shape,
        in_specs=in_specs,
        out_specs=out_specs,
        grid=grid,
        scratch_shapes=list(scratch),
        compiler_params=pltpu.CompilerParams(vmem_limit_bytes=limit * 2**20),
    )


def stack_kernel(p0, p1, p2, p3, out_ref):
    height = p0.shape[0]
    for at, piece in enumerate((p0, p1, p2, p3)):
        out_ref[at * height : (at + 1) * height, :] = piece[...]


def stack(parts):
    shape = (4 * parts[0].shape[0],) + parts[0].shape[1:]
    return call(stack_kernel, sds(shape, parts[0].dtype), [VMEM] * 4)(*parts)


def dense_kernel(index_ref, gate_ref, up_ref, down_ref, wg_ref, wu_ref, wd_ref):
    wg_ref[...] = jnp.zeros_like(wg_ref)
    wu_ref[...] = jnp.zeros_like(wu_ref)
    wd_ref[...] = jnp.zeros_like(wd_ref)

    def one(slot, carry):
        for m, (blocks, dense) in enumerate(((gate_ref, wg_ref), (up_ref, wu_ref), (down_ref, wd_ref))):
            place = index_ref[m, slot]

            @pl.when(place < SLOTS)
            def _():
                hid = pl.multiple_of(place // DB * BLK, BLK)
                feat = pl.multiple_of(place % DB * BLK, BLK)
                first, second = (hid, feat) if m == 2 else (feat, hid)
                dense[pl.ds(first, BLK), pl.ds(second, BLK)] = blocks[slot]

        return carry

    lax.fori_loop(0, CAP, one, 0)


def partial_kernel(place_ref, p0, p1, p2, p3, wg_ref, wu_ref, wd_ref, out_ref, rows, *, other):
    swap = place_ref[0] != other

    @pl.when(swap)
    def _():
        rows[:64, :] = p2[...]
        rows[64:, :] = p3[...]

    @pl.when(jnp.logical_not(swap))
    def _():
        rows[:64, :] = p0[...]
        rows[64:, :] = p1[...]

    x = rows[:, :DQ]
    dy = rows[:, DQ:]
    out_ref[:, :HB] = jnp.dot(x, wg_ref[...], preferred_element_type=F32)
    out_ref[:, HB : 2 * HB] = jnp.dot(x, wu_ref[...], preferred_element_type=F32)
    out_ref[:, 2 * HB :] = lax.dot_general(dy, wd_ref[...], NT, preferred_element_type=F32)


def pair_kernel(place_ref, keep_ref, got_ref, o0, o1, o2, o3):
    me = place_ref[1]
    lane = lax.broadcasted_iota(jnp.int32, (32, BLK), 1)
    for step, out in enumerate((o0, o1, o2, o3)):
        at = pl.ds(pl.multiple_of((me ^ step) * 32, 32), 32)
        if step == 0:
            out[...] = keep_ref[at, :] + got_ref[at, :]
            continue
        scales = jnp.zeros((32, BLK), F32)
        for m in range(3):
            part = slice(m * HB, (m + 1) * HB)
            value = keep_ref[at, part] + got_ref[at, part]
            top = jnp.max(jnp.abs(value), axis=1, keepdims=True)
            power = jnp.clip(jnp.ceil(jnp.log2(jnp.maximum(top, 1e-35))), -110.0, 120.0)
            whole = jnp.round(value * jnp.exp2(15.0 - power))
            out[:, part] = jnp.clip(whole, -32767.0, 32767.0).astype(jnp.int16)
            scales = jnp.where(lane >= m * 32, power, scales)
        out[:, 3 * HB :] = scales.astype(jnp.int16)


def act_kernel(a0, a1, a2, a3, out_ref):
    scales = [a[:, 3 * HB :].astype(F32) for a in (a1, a2, a3)]

    def total(m):
        part = slice(m * HB, (m + 1) * HB)
        value = a0[:, part]
        for a, scale in zip((a1, a2, a3), scales):
            value += a[:, part].astype(F32) * jnp.exp2(scale[:, m * 32 : m * 32 + 1] - 15.0)
        return value

    gate, up, dh = total(0), total(1), total(2)
    sig = jax.nn.sigmoid(gate)
    silu = gate * sig
    out_ref[:, :HB] = (silu * up).astype(BF)
    out_ref[:, HB : 2 * HB] = (dh * up * sig * (1.0 + gate * (1.0 - sig))).astype(BF)
    out_ref[:, 2 * HB :] = (dh * silu).astype(BF)


def spread(place_ref, mine, theirs, rows):
    core, me = place_ref[0], place_ref[1]
    for step in range(4):
        at = pl.multiple_of(core * 128 + (me ^ step) * 32, 32)
        rows[pl.ds(at, 32), :] = mine[step * 32 : (step + 1) * 32, :]
        at = pl.multiple_of((1 - core) * 128 + (me ^ step) * 32, 32)
        rows[pl.ds(at, 32), :] = theirs[step * 32 : (step + 1) * 32, :]


def out_kernel(place_ref, mine, theirs, wg_ref, wu_ref, wd_ref, t0, t1, t2, t3, full_ref):
    spread(place_ref, mine, theirs, full_ref)
    mixed = jnp.dot(full_ref[:, :HB], wd_ref[...], preferred_element_type=F32)
    for step, out in enumerate((t0, t1, t2, t3)):
        out[:, :DQ] = mixed[step * 64 : (step + 1) * 64].astype(out.dtype)
    grad = lax.dot_general(full_ref[:, HB : 2 * HB], wg_ref[...], NT, preferred_element_type=F32)
    grad += lax.dot_general(full_ref[:, 2 * HB :], wu_ref[...], NT, preferred_element_type=F32)
    for step, out in enumerate((t0, t1, t2, t3)):
        out[:, DQ:] = grad[step * 64 : (step + 1) * 64].astype(out.dtype)


def prep_kernel(p0, p1, p2, p3, out_ref):
    for b in range(DB):
        for side, pair in enumerate(((p0, p1), (p2, p3))):
            lanes = slice(side * 128, (side + 1) * 128)
            x = jnp.concatenate([p[:, b * BLK : (b + 1) * BLK] for p in pair], axis=0)
            out_ref[b, :, lanes] = x.T
            for low, p in enumerate(pair):
                out_ref[DB + b, low * 64 : (low + 1) * 64, lanes] = p[:, DQ + b * BLK : DQ + (b + 1) * BLK]


def grad_kernel(code_ref, full, s0, s1, s2, s3, out_ref, slab, ht, dg, du):
    turn = pl.program_id(0)

    @pl.when(turn == 0)
    def _():
        for j, source in enumerate((s0, s1, s2, s3)):
            slab[j * 2 * DB : (j + 1) * 2 * DB] = source[...]
        for a in range(FB):
            ht[a] = full[:, a * BLK : (a + 1) * BLK].T
            dg[a] = full[:, HB + a * BLK : HB + (a + 1) * BLK]
            du[a] = full[:, 2 * HB + a * BLK : 2 * HB + (a + 1) * BLK]

    for near in range(STEP):
        for m in range(3):
            code = code_ref[m, turn * STEP + near]
            where = jnp.maximum(code - 1, 0)
            feat = where // 64 * 2 * DB + where % 8
            hid = where % 64 // 8
            if m == 2:
                left = ht[hid]
                right = jnp.concatenate([slab[feat + DB, :, :128], slab[feat + DB, :, 128:]], axis=0)
            else:
                left = slab[feat]
                right = (dg, du)[m][hid]
            value = jnp.dot(left, right, preferred_element_type=F32)
            out_ref[m, near] = jnp.where(code > 0, value, 0.0).astype(BF)


def body(activations, out_grad, gate_blocks, up_blocks, down_blocks, block_index, block_dest):
    row = lax.axis_index("row")
    col = lax.axis_index("col")
    group = row // QUARTERS
    quarter = row % QUARTERS
    place = jnp.stack([row % 2, row // 2 % 2 * 2 + col]).astype(jnp.int32)
    all_index = lax.dynamic_index_in_dim(block_index, col, axis=2, keepdims=False)
    own_index = lax.dynamic_index_in_dim(all_index, row, axis=1, keepdims=False)

    tie = lax.optimization_barrier
    shard = jnp.concatenate([activations, out_grad], axis=1)
    pair = jnp.concatenate([shard, row_swap(shard, Y_MASK)], axis=0)
    near = stack([pair] + [row_swap(pair, z_mask(i)) for i in ORDER])
    pieces = [near] + [row_swap(near, x_mask(i)) for i in ORDER]
    halves = [row_swap(near[at * 32 : (at + 1) * 32], 2) for at in range(2)]

    wide = [sds((DQ, HB), BF), sds((DQ, HB), BF), sds((HB, DQ), BF)]
    wg, wu, wd = call(dense_kernel, wide, [SMEM] + [VMEM] * 3)(
        own_index,
        gate_blocks.reshape(CAP, BLK, BLK),
        up_blocks.reshape(CAP, BLK, BLK),
        down_blocks.reshape(CAP, BLK, BLK),
    )
    dest = lax.dynamic_slice_in_dim(block_dest[:, :, 0, :], group * QUARTERS, QUARTERS, axis=1)
    index = lax.dynamic_slice_in_dim(all_index, group * QUARTERS, QUARTERS, axis=1)
    swap = (jnp.arange(QUARTERS, dtype=jnp.int32) ^ quarter)[None, :, None]
    value = (swap * 64 + index + 1).reshape(3, 1, QUARTERS * CAP)
    targets = quarter * CAP + jnp.arange(CAP, dtype=jnp.int32)
    hits = dest.reshape(3, 1, QUARTERS * CAP) == targets[None, :, None]
    code = jnp.sum(jnp.where(hits, value, 0), axis=2, dtype=jnp.int32)
    pieces, halves, code = tie((pieces, halves, code))
    mirror = jnp.concatenate(halves, axis=0)

    half = sds((128, 3 * HB), F32)

    def partial(other):
        return call(
            functools.partial(partial_kernel, other=other),
            half,
            [SMEM] + [VMEM] * 7,
            scratch=[pltpu.VMEM((128, 2 * DQ), BF)],
        )(place, *pieces, wg, wu, wd)

    send = partial(1)
    got = row_swap(send, 1)
    keep = partial(0)
    coded = sds((32, 3 * HB + BLK), jnp.int16)
    sums = call(pair_kernel, [sds((32, 3 * HB), F32)] + [coded] * 3, [SMEM, VMEM, VMEM])(place, keep, got)
    sums = [sums[0]] + [square_swap(sums[i], i) for i in (3, 1, 2)]

    prep = call(prep_kernel, sds((2 * DB, BLK, TOKENS), BF), [VMEM] * 4)
    mirror, keep = tie((mirror, keep))
    mirror1, mirror2, mirror3 = [row_swap(mirror, x_mask(i)) for i in ORDER]
    slab0 = prep(*tie((pieces, sums[0]))[0])
    sums, mirror1, slab0 = tie((sums, mirror1, slab0))
    share = call(act_kernel, sds((32, 3 * HB), BF), [VMEM] * 4)(*sums)
    mine = [share] + [square_swap(share, i) for i in range(1, 4)]
    slab1 = row_swap(slab0, 1)
    mine, mirror2, mirror3 = tie((mine, mirror2, mirror3))
    mine = jnp.concatenate(mine, axis=0)
    theirs = row_swap(mine, 1)
    slab2 = prep(mirror, mirror1, mirror2, mirror3)
    theirs, slab2, slab1 = tie((theirs, slab2, slab1))
    outs = call(
        out_kernel,
        [sds((64, 2 * DQ), F32)] + [sds((64, 2 * DQ), BF)] * 3 + [sds((TOKENS, 3 * HB), BF)],
        [SMEM] + [VMEM] * 5,
    )(place, mine, theirs, wg, wu, wd)
    full = outs[4]
    slab2, full = tie((slab2, full))
    slab3 = row_swap(slab2, 1)
    far3, far1, far2 = [row_swap(outs[at], x_mask(ORDER[at - 1])) for at in (3, 1, 2)]

    grads = call(
        grad_kernel,
        sds((3, CAP, BLK, BLK), BF),
        [SMEM] + [VMEM] * 5,
        out_specs=pl.BlockSpec((3, STEP, BLK, BLK), lambda i: (0, i, 0, 0)),
        scratch=[
            pltpu.VMEM((QUARTERS * 2 * DB, BLK, TOKENS), BF),
            pltpu.VMEM((FB, BLK, TOKENS), BF),
            pltpu.VMEM((FB, TOKENS, BLK), BF),
            pltpu.VMEM((FB, TOKENS, BLK), BF),
        ],
        grid=(CAP // STEP,),
        limit=24,
    )(code, full, slab0, slab1, slab2, slab3)
    far3, far1, far2, grads = tie((far3, far1, far2, grads))
    total = outs[0] + far3.astype(F32) + far1.astype(F32) + far2.astype(F32)
    last = total[: 2 * TG]
    for at in (3, 1, 2):
        part = total[at * 2 * TG : (at + 1) * 2 * TG].astype(BF)
        last = last + row_swap(part, z_mask(ORDER[at - 1])).astype(F32)
    got = row_swap(last[TG:].astype(BF), Y_MASK).astype(F32)
    mixed_rows, input_grad = [(last[:TG, c] + got[:, c]).astype(BF) for c in (slice(0, DQ), slice(DQ, 2 * DQ))]
    return mixed_rows, input_grad, grads.reshape(3, 1, 1, CAP, BLK, BLK)


def solution(mesh):
    return jax.shard_map(
        body,
        mesh=mesh,
        in_specs=(
            P("row", "col"),
            P("row", "col"),
            P("row", "col", None, None, None),
            P("row", "col", None, None, None),
            P("row", "col", None, None, None),
            P(),
            P(None, None, "col", None),
        ),
        out_specs=(P("row", "col"), P("row", "col"), P(None, "row", "col", None, None, None)),
        check_vma=False,
    )
```

```python
import functools

import jax
import jax.numpy as jnp
from jax import lax
from jax.experimental import pallas as pl
from jax.experimental.pallas import tpu as pltpu
from jax.sharding import PartitionSpec as P

BLK = 128
QUARTERS = 4
FB = 7
DB = 8
SLOTS = 56
CAP = 48
DQ = 1024
HB = 896
TG = 8
STEP = 8
TOKENS = 256
ORDER = (1, 3, 2)
BF = jnp.bfloat16
F32 = jnp.float32
NT = (((1,), (1,)), ((), ()))
VMEM = pl.BlockSpec(memory_space=pltpu.VMEM)
SMEM = pl.BlockSpec(memory_space=pltpu.SMEM)


def row_swap(value, mask):
    return lax.ppermute(value, "row", [(i, i ^ mask) for i in range(128)])


def square_swap(value, step):
    mask = (step >> 1) * 4 | (step & 1)
    return lax.ppermute(value, ("row", "col"), [(i, i ^ mask) for i in range(256)])


def z_mask(step):
    return step << 2


Y_MASK = 64


def x_mask(step):
    return step << 4


def sds(shape, dtype):
    return jax.ShapeDtypeStruct(shape, dtype)


def call(kernel, out_shape, in_specs, out_specs=None, scratch=(), limit=16, grid=()):
    many = isinstance(out_shape, (tuple, list))
    if out_specs is None:
        out_specs = [VMEM] * len(out_shape) if many else VMEM
    return pl.pallas_call(
        kernel,
        out_shape=out_shape,
        in_specs=in_specs,
        out_specs=out_specs,
        grid=grid,
        scratch_shapes=list(scratch),
        compiler_params=pltpu.CompilerParams(vmem_limit_bytes=limit * 2**20),
    )


def stack_kernel(p0, p1, p2, p3, out_ref):
    height = p0.shape[0]
    for at, piece in enumerate((p0, p1, p2, p3)):
        out_ref[at * height : (at + 1) * height, :] = piece[...]


def stack(parts):
    shape = (4 * parts[0].shape[0],) + parts[0].shape[1:]
    return call(stack_kernel, sds(shape, parts[0].dtype), [VMEM] * 4)(*parts)


def dense_kernel(index_ref, gate_ref, up_ref, down_ref, wg_ref, wu_ref, wd_ref):
    wg_ref[...] = jnp.zeros_like(wg_ref)
    wu_ref[...] = jnp.zeros_like(wu_ref)
    wd_ref[...] = jnp.zeros_like(wd_ref)

    def one(slot, carry):
        for m, (blocks, dense) in enumerate(((gate_ref, wg_ref), (up_ref, wu_ref), (down_ref, wd_ref))):
            place = index_ref[m, slot]

            @pl.when(place < SLOTS)
            def _():
                hid = pl.multiple_of(place // DB * BLK, BLK)
                feat = pl.multiple_of(place % DB * BLK, BLK)
                first, second = (hid, feat) if m == 2 else (feat, hid)
                dense[pl.ds(first, BLK), pl.ds(second, BLK)] = blocks[slot]

        return carry

    lax.fori_loop(0, CAP, one, 0)


def partial_kernel(place_ref, p0, p1, p2, p3, wg_ref, wu_ref, wd_ref, out_ref, rows, *, other):
    swap = place_ref[0] != other

    @pl.when(swap)
    def _():
        rows[:64, :] = p2[...]
        rows[64:, :] = p3[...]

    @pl.when(jnp.logical_not(swap))
    def _():
        rows[:64, :] = p0[...]
        rows[64:, :] = p1[...]

    x = rows[:, :DQ]
    dy = rows[:, DQ:]
    out_ref[:, :HB] = jnp.dot(x, wg_ref[...], preferred_element_type=F32)
    out_ref[:, HB : 2 * HB] = jnp.dot(x, wu_ref[...], preferred_element_type=F32)
    out_ref[:, 2 * HB :] = lax.dot_general(dy, wd_ref[...], NT, preferred_element_type=F32)


def pair_kernel(place_ref, keep_ref, got_ref, o0, o1, o2, o3):
    me = place_ref[1]
    lane = lax.broadcasted_iota(jnp.int32, (32, BLK), 1)
    for step, out in enumerate((o0, o1, o2, o3)):
        at = pl.ds(pl.multiple_of((me ^ step) * 32, 32), 32)
        if step == 0:
            out[...] = keep_ref[at, :] + got_ref[at, :]
            continue
        scales = jnp.zeros((32, BLK), F32)
        for m in range(3):
            part = slice(m * HB, (m + 1) * HB)
            value = keep_ref[at, part] + got_ref[at, part]
            top = jnp.max(jnp.abs(value), axis=1, keepdims=True)
            power = jnp.clip(jnp.ceil(jnp.log2(jnp.maximum(top, 1e-35))), -110.0, 120.0)
            whole = jnp.round(value * jnp.exp2(15.0 - power))
            out[:, part] = jnp.clip(whole, -32767.0, 32767.0).astype(jnp.int16)
            scales = jnp.where(lane >= m * 32, power, scales)
        out[:, 3 * HB :] = scales.astype(jnp.int16)


def act_kernel(a0, a1, a2, a3, out_ref):
    scales = [a[:, 3 * HB :].astype(F32) for a in (a1, a2, a3)]

    def total(m):
        part = slice(m * HB, (m + 1) * HB)
        value = a0[:, part]
        for a, scale in zip((a1, a2, a3), scales):
            value += a[:, part].astype(F32) * jnp.exp2(scale[:, m * 32 : m * 32 + 1] - 15.0)
        return value

    gate, up, dh = total(0), total(1), total(2)
    sig = jax.nn.sigmoid(gate)
    silu = gate * sig
    out_ref[:, :HB] = (silu * up).astype(BF)
    out_ref[:, HB : 2 * HB] = (dh * up * sig * (1.0 + gate * (1.0 - sig))).astype(BF)
    out_ref[:, 2 * HB :] = (dh * silu).astype(BF)


def spread(place_ref, mine, theirs, rows):
    core, me = place_ref[0], place_ref[1]
    for step in range(4):
        at = pl.multiple_of(core * 128 + (me ^ step) * 32, 32)
        rows[pl.ds(at, 32), :] = mine[step * 32 : (step + 1) * 32, :]
        at = pl.multiple_of((1 - core) * 128 + (me ^ step) * 32, 32)
        rows[pl.ds(at, 32), :] = theirs[step * 32 : (step + 1) * 32, :]


def out_kernel(place_ref, mine, theirs, wg_ref, wu_ref, wd_ref, t0, t1, t2, t3, full_ref):
    spread(place_ref, mine, theirs, full_ref)
    mixed = jnp.dot(full_ref[:, :HB], wd_ref[...], preferred_element_type=F32)
    for step, out in enumerate((t0, t1, t2, t3)):
        out[:, :DQ] = mixed[step * 64 : (step + 1) * 64].astype(out.dtype)
    grad = lax.dot_general(full_ref[:, HB : 2 * HB], wg_ref[...], NT, preferred_element_type=F32)
    grad += lax.dot_general(full_ref[:, 2 * HB :], wu_ref[...], NT, preferred_element_type=F32)
    for step, out in enumerate((t0, t1, t2, t3)):
        out[:, DQ:] = grad[step * 64 : (step + 1) * 64].astype(out.dtype)


def prep_kernel(p0, p1, p2, p3, out_ref):
    for b in range(DB):
        for side, pair in enumerate(((p0, p1), (p2, p3))):
            lanes = slice(side * 128, (side + 1) * 128)
            x = jnp.concatenate([p[:, b * BLK : (b + 1) * BLK] for p in pair], axis=0)
            out_ref[b, :, lanes] = x.T
            for low, p in enumerate(pair):
                out_ref[DB + b, low * 64 : (low + 1) * 64, lanes] = p[:, DQ + b * BLK : DQ + (b + 1) * BLK]


def grad_kernel(code_ref, full, s0, s1, s2, s3, out_ref, slab, ht, dg, du):
    turn = pl.program_id(0)

    @pl.when(turn == 0)
    def _():
        for j, source in enumerate((s0, s1, s2, s3)):
            slab[j * 2 * DB : (j + 1) * 2 * DB] = source[...]
        for a in range(FB):
            ht[a] = full[:, a * BLK : (a + 1) * BLK].T
            dg[a] = full[:, HB + a * BLK : HB + (a + 1) * BLK]
            du[a] = full[:, 2 * HB + a * BLK : 2 * HB + (a + 1) * BLK]

    for near in range(STEP):
        for m in range(3):
            code = code_ref[m, turn * STEP + near]
            where = jnp.maximum(code - 1, 0)
            feat = where // 64 * 2 * DB + where % 8
            hid = where % 64 // 8
            if m == 2:
                left = ht[hid]
                right = jnp.concatenate([slab[feat + DB, :, :128], slab[feat + DB, :, 128:]], axis=0)
            else:
                left = slab[feat]
                right = (dg, du)[m][hid]
            value = jnp.dot(left, right, preferred_element_type=F32)
            out_ref[m, near] = jnp.where(code > 0, value, 0.0).astype(BF)


def body(activations, out_grad, gate_blocks, up_blocks, down_blocks, block_index, block_dest):
    row = lax.axis_index("row")
    col = lax.axis_index("col")
    group = row // QUARTERS
    quarter = row % QUARTERS
    place = jnp.stack([row % 2, row // 2 % 2 * 2 + col]).astype(jnp.int32)
    all_index = lax.dynamic_index_in_dim(block_index, col, axis=2, keepdims=False)
    own_index = lax.dynamic_index_in_dim(all_index, row, axis=1, keepdims=False)

    tie = lax.optimization_barrier
    shard = jnp.pad(activations, ((0, 0), (0, DQ))) + jnp.pad(out_grad, ((0, 0), (DQ, 0)))
    pair = jnp.concatenate([shard, row_swap(shard, Y_MASK)], axis=0)
    near = stack([pair] + [row_swap(pair, z_mask(i)) for i in ORDER])
    pieces = [near] + [row_swap(near, x_mask(i)) for i in ORDER]
    halves = [row_swap(near[at * 32 : (at + 1) * 32], 2) for at in range(2)]

    wide = [sds((DQ, HB), BF), sds((DQ, HB), BF), sds((HB, DQ), BF)]
    wg, wu, wd = call(dense_kernel, wide, [SMEM] + [VMEM] * 3)(
        own_index,
        gate_blocks.reshape(CAP, BLK, BLK),
        up_blocks.reshape(CAP, BLK, BLK),
        down_blocks.reshape(CAP, BLK, BLK),
    )
    dest = lax.dynamic_slice_in_dim(block_dest[:, :, 0, :], group * QUARTERS, QUARTERS, axis=1)
    index = lax.dynamic_slice_in_dim(all_index, group * QUARTERS, QUARTERS, axis=1)
    swap = (jnp.arange(QUARTERS, dtype=jnp.int32) ^ quarter)[None, :, None]
    value = (swap * 64 + index + 1).reshape(3, 1, QUARTERS * CAP)
    targets = quarter * CAP + jnp.arange(CAP, dtype=jnp.int32)
    hits = dest.reshape(3, 1, QUARTERS * CAP) == targets[None, :, None]
    code = jnp.sum(jnp.where(hits, value, 0), axis=2, dtype=jnp.int32)
    pieces, halves, code = tie((pieces, halves, code))
    mirror = jnp.concatenate(halves, axis=0)

    half = sds((128, 3 * HB), F32)

    def partial(other):
        return call(
            functools.partial(partial_kernel, other=other),
            half,
            [SMEM] + [VMEM] * 7,
            scratch=[pltpu.VMEM((128, 2 * DQ), BF)],
        )(place, *pieces, wg, wu, wd)

    send = partial(1)
    got = row_swap(send, 1)
    keep = partial(0)
    coded = sds((32, 3 * HB + BLK), jnp.int16)
    sums = call(pair_kernel, [sds((32, 3 * HB), F32)] + [coded] * 3, [SMEM, VMEM, VMEM])(place, keep, got)
    sums = [sums[0]] + [square_swap(sums[i], i) for i in (3, 1, 2)]

    prep = call(prep_kernel, sds((2 * DB, BLK, TOKENS), BF), [VMEM] * 4)
    mirror, keep = tie((mirror, keep))
    mirror1, mirror2, mirror3 = [row_swap(mirror, x_mask(i)) for i in ORDER]
    slab0 = prep(*tie((pieces, sums[0]))[0])
    sums, mirror1, slab0 = tie((sums, mirror1, slab0))
    share = call(act_kernel, sds((32, 3 * HB), BF), [VMEM] * 4)(*sums)
    mine = [share] + [square_swap(share, i) for i in range(1, 4)]
    slab1 = row_swap(slab0, 1)
    mine, mirror2, mirror3 = tie((mine, mirror2, mirror3))
    mine = jnp.concatenate(mine, axis=0)
    theirs = row_swap(mine, 1)
    slab2 = prep(mirror, mirror1, mirror2, mirror3)
    theirs, slab2, slab1 = tie((theirs, slab2, slab1))
    outs = call(
        out_kernel,
        [sds((64, 2 * DQ), F32)] + [sds((64, 2 * DQ), BF)] * 3 + [sds((TOKENS, 3 * HB), BF)],
        [SMEM] + [VMEM] * 5,
    )(place, mine, theirs, wg, wu, wd)
    full = outs[4]
    slab2, full = tie((slab2, full))
    slab3 = row_swap(slab2, 1)
    far3, far1, far2 = [row_swap(outs[at], x_mask(ORDER[at - 1])) for at in (3, 1, 2)]

    grads = call(
        grad_kernel,
        sds((3, CAP, BLK, BLK), BF),
        [SMEM] + [VMEM] * 5,
        out_specs=pl.BlockSpec((3, STEP, BLK, BLK), lambda i: (0, i, 0, 0)),
        scratch=[
            pltpu.VMEM((QUARTERS * 2 * DB, BLK, TOKENS), BF),
            pltpu.VMEM((FB, BLK, TOKENS), BF),
            pltpu.VMEM((FB, TOKENS, BLK), BF),
            pltpu.VMEM((FB, TOKENS, BLK), BF),
        ],
        grid=(CAP // STEP,),
        limit=24,
    )(code, full, slab0, slab1, slab2, slab3)
    far3, far1, far2, grads = tie((far3, far1, far2, grads))
    total = outs[0] + far3.astype(F32) + far1.astype(F32) + far2.astype(F32)
    last = total[: 2 * TG]
    for at in (3, 1, 2):
        part = total[at * 2 * TG : (at + 1) * 2 * TG].astype(BF)
        last = last + row_swap(part, z_mask(ORDER[at - 1])).astype(F32)
    got = row_swap(last[TG:].astype(BF), Y_MASK)
    mixed_rows, input_grad = [
        (last[:TG, c] + got[:, c].astype(F32)).astype(BF) for c in (slice(0, DQ), slice(DQ, 2 * DQ))
    ]
    return mixed_rows, input_grad, grads.reshape(3, 1, 1, CAP, BLK, BLK)


def solution(mesh):
    return jax.shard_map(
        body,
        mesh=mesh,
        in_specs=(
            P("row", "col"),
            P("row", "col"),
            P("row", "col", None, None, None),
            P("row", "col", None, None, None),
            P("row", "col", None, None, None),
            P(),
            P(None, None, "col", None),
        ),
        out_specs=(P("row", "col"), P("row", "col"), P(None, "row", "col", None, None, None)),
        check_vma=False,
    )
```
